128 devices in a mesh: mesh: 2 (over core), blk: 64 (over y, x, z).
Axes of the slice: x: 4, y: 4, z: 4, core: 2. Of those that a mesh axis runs over, the one named last changes fastest.
Arguments:
- rotation_step: int32 [1], replicated, may hold values from 1 to 7
- field_state: float32 [2, 64, 4, 128, 256], P('mesh', 'blk'), may hold values from -6 to 6
- diffusivity: float32 [2, 64, 2, 128, 256], P('mesh', 'blk'), may hold values from 0.05 to 2
- stretch: float32 [2, 64, 128, 256], P('mesh', 'blk'), may hold values from 100 to 3000
- donor_base: int32 [2, 64, 4096], P('mesh', 'blk'), may hold values from 0 to 32478, as said below
- donor_frac: float32 [2, 64, 3, 4096], P('mesh', 'blk'), may hold values from 0 to 1
- fringe_cell: int32 [2, 64, 4096], P('mesh', 'blk'), may hold values from 0 to 32768, as said below
Outputs:
- new_fields: float32 [2, 64, 4, 128, 256], P('mesh', 'blk')
The draws below stay inside these ranges and needn't reach their ends.
Inputs may be any that keep to these rules, and one draw needn't show every extreme that they name: `donor_base`: each entry is z * 8 * 32 + x * 32 + y with z < 127, x < 7 and y < 31. `fringe_cell`: in each block, the slots p * 64 to (p + 1) * 64 - 1 hold the cells that receive values from block p of the other mesh, used slots first; every fringe cell of the block is named by exactly one used slot; an unused slot holds 32768. A group has 0 to 64 used slots, and in every block some group is full and some is empty.
All inputs are finite; a program needn't handle non-finite values.
Results may differ from the reference program's by a relative error of at most 0.00017.
Values sent between devices are 32-bit elements; how exact they have to be, the bound alone decides.
A program may use at most 64 MiB of HBM per device.

```python
import math
from functools import partial
import jax
import jax.numpy as jnp
from jax import lax

CX = 8
CY = 32
CZ = 128
ITERS = 2
TURN_MOST = 7
NB = 64
SLOTS = 4096
CAP = 64


def fringe_block(block_key):
    key_pair, key_shift, key_cells = jax.random.split(block_key, 3)
    half_cap = CAP // 2
    pairing = jax.random.permutation(key_pair, NB)
    transfer = jax.random.randint(key_shift, (NB // 2,), 0, half_cap + 1)
    transfer = transfer.at[0].set(half_cap)
    counts = jnp.zeros((NB,), jnp.int32)
    counts = counts.at[pairing[0::2]].set(half_cap + transfer)
    counts = counts.at[pairing[1::2]].set(half_cap - transfer)
    offsets = jnp.cumsum(counts) - counts
    slot_ids = jnp.arange(SLOTS, dtype=jnp.int32)
    group_ids = slot_ids // CAP
    within = slot_ids % CAP
    is_live = within < counts[group_ids]
    ranks = jnp.minimum(offsets[group_ids] + within, SLOTS // 2 - 1)
    shuffled = jax.random.permutation(key_cells, SLOTS // 2)
    picked = shuffled[ranks]
    depth = picked // (2 * CX)
    remains = picked % (2 * CX)
    row_pos = remains // 2
    col_pos = remains % 2 * (CY - 1)
    flat_cell = depth * CX * CY + row_pos * CY + col_pos
    return jnp.where(is_live, flat_cell, CZ * CX * CY).astype(jnp.int32)


def draw_fringe_cell(key, part):
    block_keys = jax.vmap(lambda index_value: jax.random.fold_in(key, index_value))(jnp.arange(2 * NB))
    return jax.vmap(fringe_block)(block_keys).reshape(2, NB, SLOTS)


def draw_donor_base(key, part):
    key_depth, key_row, key_col = jax.random.split(jax.random.fold_in(key, 7), 3)
    shape_all = (2, NB, SLOTS)
    depth = jax.random.randint(key_depth, shape_all, 0, CZ - 1)
    row_pos = jax.random.randint(key_row, shape_all, 0, CX - 1)
    col_pos = jax.random.randint(key_col, shape_all, 0, CY - 1)
    flat_cell = depth * CX * CY + row_pos * CY + col_pos
    flat_cell = flat_cell.at[0, 0, 0].set((CZ - 2) * CX * CY + (CX - 2) * CY + CY - 2)
    return flat_cell.astype(jnp.int32)


def steps_of(own_key, shape, cuts, low, top_value):
    loudness, own = 1.0, jax.random.fold_in(own_key, 6)
    for position, shards_of in cuts:
        steps = jnp.exp(jax.random.uniform(jax.random.fold_in(own, position), (shards_of,), jnp.float32, low / len(cuts), top_value / len(cuts)))
        loudness = loudness * jnp.repeat(steps, shape[position] // shards_of).reshape([-1 if axis == position else 1 for axis in range(len(shape))])
    return loudness


def centred(key, shape, deviation, bound, pieces=(), kind=jnp.bfloat16):
    array = jax.random.normal(key, shape, jnp.float32) * deviation
    if len(pieces) > 0:
        array = steps_of(key, shape, pieces, -0.22, 0.18) * array
    return jnp.clip(array, min=-bound, max=bound).astype(kind)


def setup_inputs(seed: int = 0) -> dict:
    streams_of = jax.random.split(jax.random.key(seed), 8)
    rotation_step = jax.random.randint(streams_of[0], (1,), 1, TURN_MOST + 1).astype(jnp.int32)
    field_state = centred(streams_of[1], (2, NB, 4, CZ, CX * CY), 1.0, 6.0, ((0, 2), (1, 64)), jnp.float32)
    diffusivity = jnp.clip(jnp.exp(math.log(2.0) - 3.6888794 * jax.random.uniform(streams_of[2], (2, NB, 2, CZ, CX * CY), jnp.float32) ** steps_of(streams_of[2], (2, NB, 2, CZ, CX * CY), ((0, 2), (1, 64)), -0.2, 0.2)), 0.05, 2.0)
    stretch = jnp.clip(jnp.exp(math.log(3000.0) - 3.4011974 * jax.random.uniform(streams_of[3], (2, NB, CZ, CX * CY), jnp.float32) ** steps_of(streams_of[3], (2, NB, CZ, CX * CY), ((0, 2), (1, 64)), -0.2, 0.2)), 100.0, 3000.0)
    donor_base = draw_donor_base(jax.random.fold_in(streams_of[7], 71), 0)
    donor_frac = jnp.clip(1.0 * jax.random.uniform(streams_of[5], (2, NB, 3, SLOTS), jnp.float32) ** steps_of(streams_of[5], (2, NB, 3, SLOTS), ((0, 2), (1, 64)), -0.2, 0.2), 0.0, 1.0)
    fringe_cell = draw_fringe_cell(jax.random.fold_in(streams_of[7], 71), 0)
    return {"rotation_step": rotation_step, "field_state": field_state, "diffusivity": diffusivity, "stretch": stretch, "donor_base": donor_base, "donor_frac": donor_frac, "fringe_cell": fringe_cell}


def before(values, stride, filler):
    length = values.shape[-2]
    padding = jnp.full(values.shape[:-2] + (stride,) + values.shape[-1:], filler, values.dtype)
    return jnp.concatenate([padding, values[..., :length - stride, :]], axis=-2)


def behind(values, stride, filler):
    length = values.shape[-2]
    padding = jnp.full(values.shape[:-2] + (stride,) + values.shape[-1:], filler, values.dtype)
    return jnp.concatenate([values[..., stride:, :], padding], axis=-2)


def solve_lines(lower_band, middle, upper_band, right_side):
    length = middle.shape[-2]
    stride = 1
    while stride < length:
        factor_low = -lower_band / before(middle, stride, 1.0)
        factor_high = -upper_band / behind(middle, stride, 1.0)
        new_lower = factor_low * before(lower_band, stride, 0.0)
        new_upper = factor_high * behind(upper_band, stride, 0.0)
        new_middle = middle + factor_low * before(upper_band, stride, 0.0) + factor_high * behind(lower_band, stride, 0.0)
        new_right = right_side + factor_low * before(right_side, stride, 0.0) + factor_high * behind(right_side, stride, 0.0)
        lower_band, upper_band, middle, right_side = new_lower, new_upper, new_middle, new_right
        stride = stride * 2
    return right_side / middle


def interpolate(fields, donor_bases, donor_fracs, row_length):
    plane_size = fields.shape[-1]
    flattened = fields.reshape(fields.shape[0], -1)
    summed = jnp.zeros((fields.shape[0], donor_bases.shape[-1]), fields.dtype)
    for depth_step in (0, 1):
        weight_z = donor_fracs[0] if depth_step else 1.0 - donor_fracs[0]
        for row_step in (0, 1):
            weight_x = donor_fracs[1] if row_step else 1.0 - donor_fracs[1]
            for col_step in (0, 1):
                weight_y = donor_fracs[2] if col_step else 1.0 - donor_fracs[2]
                offset = depth_step * plane_size + row_step * row_length + col_step
                picked = jnp.take(flattened, donor_bases + offset, axis=1)
                summed = summed + (weight_z * weight_x * weight_y)[None, :] * picked
    return summed


def place_donors(fields, target_cells, arrived):
    flattened = fields.reshape(fields.shape[0], -1)
    flattened = flattened.at[:, target_cells].set(arrived, mode="drop")
    return flattened.reshape(fields.shape)


def relax_block(filled, extended, initial, coeffs, along):
    width = filled.shape[-1]
    rim_width = (extended.shape[-1] - width) // 2
    across = extended[..., :width] + extended[..., 2 * rim_width:]
    zero_column = jnp.zeros(filled.shape[:-1] + (1,), filled.dtype)
    sideways = jnp.concatenate([zero_column, filled[..., :-1]], axis=-1) + jnp.concatenate([filled[..., 1:], zero_column], axis=-1)
    per_field = jnp.concatenate([coeffs[0:1], coeffs[0:1], coeffs[0:1], coeffs[1:2]], axis=0)
    right_side = initial + per_field * (across + sideways)
    along_full = jnp.broadcast_to(along[None], filled.shape)
    middle = 1.0 + 2.0 * along_full + 4.0 * per_field
    depth_index = lax.broadcasted_iota(jnp.int32, filled.shape, 1)
    lower_band = jnp.where(depth_index == 0, 0.0, -along_full)
    upper_band = jnp.where(depth_index == filled.shape[1] - 1, 0.0, -along_full)
    solved = solve_lines(lower_band, middle, upper_band, right_side)
    column = lax.broadcasted_iota(jnp.int32, filled.shape, 2) % rim_width
    fringe = (column == 0) | (column == rim_width - 1)
    return jnp.where(fringe, filled, solved)


def reference(rotation_step, field_state, diffusivity, stretch, donor_base, donor_frac, fringe_cell):
    rotation = rotation_step[0]

    def migrate(values):
        return jnp.stack([values[0], jnp.roll(values[1], rotation, axis=0)])

    initial = migrate(field_state)
    coeffs = migrate(diffusivity)
    alongs = migrate(stretch)
    donor_bases = migrate(donor_base)
    donor_fracs = migrate(donor_frac)
    target_cells = migrate(fringe_cell)
    blocks = field_state.shape[1]
    per_peer = target_cells.shape[-1] // blocks
    fields = initial
    inner = jax.vmap(jax.vmap(partial(interpolate, row_length=CY)))
    placing = jax.vmap(jax.vmap(place_donors))
    for sweep_index in range(ITERS):
        outbound = inner(fields, donor_bases, donor_fracs)
        grouped = outbound.reshape(2, blocks, 4, blocks, per_peer).transpose(0, 3, 2, 1, 4)
        grouped = grouped.reshape(2, blocks, 4, blocks * per_peer)[::-1]
        filled = placing(fields, target_cells, grouped)
        left_rim = jnp.roll(filled, 1, axis=1)[..., -CY:]
        right_rim = jnp.roll(filled, -1, axis=1)[..., :CY]
        extended = jnp.concatenate([left_rim, filled, right_rim], axis=-1)
        flat_shape = (2 * blocks,)

        def relax_one(packed):
            return relax_block(packed[0], packed[1], packed[2], packed[3], packed[4])

        relaxed = lax.map(relax_one, (filled.reshape(flat_shape + filled.shape[2:]), extended.reshape(flat_shape + extended.shape[2:]), initial.reshape(flat_shape + initial.shape[2:]), coeffs.reshape(flat_shape + coeffs.shape[2:]), alongs.reshape(flat_shape + alongs.shape[2:])))
        fields = relaxed.reshape(filled.shape)
    return fields
```

```python
import functools

import jax
import jax.numpy as jnp
from jax import lax
from jax.experimental import pallas as pl
from jax.experimental.pallas import tpu as pltpu
from jax.sharding import PartitionSpec as P

CX, CY, CZ = 8, 32, 128
PLANE = CX * CY
ITERS = 2
TURN_MOST = 7
CAP = 64
TILE = 256
LANES = 128
MESH = pl.DeviceIdType.MESH
BF = jnp.bfloat16
F32 = jnp.float32


def iota(shape, dim):
    return lax.broadcasted_iota(jnp.int32, shape, dim)


def kernel(
    rot, n,
    fs, kap, st, db, df, fc, out,
    F0, KV, SV, SB, SF, SC, A3, W3, WZ, ZO, QO, QV, E, NN, V2,
    EP, CS, IN, R, G, D, FR, NS, OUT,
    sendS, recvS, sendH, recvH,
    in_sem, s_sem, r_sem, hs_sem, hr_sem, m_sem, o_sem,
):
    m = lax.axis_index("mesh")
    d = lax.axis_index("blk")
    slots = n * CAP
    tiles = slots // TILE
    right, left = lax.rem(d + 1, n), lax.rem(d + n - 1, n)
    ahead, back = lax.rem(d + rot, n), lax.rem(d + n - rot, n)

    loads = [
        pltpu.make_async_copy(src, dst, in_sem.at[i])
        for i, (src, dst) in enumerate(((db, SB), (df, SF), (fc, SC), (fs, F0), (kap, KV), (st, SV)))
    ]
    for copy in loads:
        copy.start()

    barrier = pltpu.get_barrier_semaphore()

    @pl.loop(0, n)
    def _(i):
        pl.semaphore_signal(barrier, inc=1, device_id=(1 - m, lax.rem(d + i, n)), device_id_type=MESH)

    for peer in (left, right, ahead, back):
        pl.semaphore_signal(barrier, inc=1, device_id=(m, peer), device_id_type=MESH)

    row, col = iota((192, 2 * 2 * 4 * LANES), 0), iota((192, 2 * 2 * 4 * LANES), 1)
    q = row % 16
    kind, half, fld, lane = col // 1024, (col // 512) % 2, (col // 128) % 4, col % 128
    place = (q >> 1) * CY + (q & 1) * (CY - 1) + kind * (1 - 2 * (q & 1))
    E[...] = jnp.where(((row // 16) % 4 == fld) & (half * LANES + lane == place), 1.0, 0.0).astype(BF)
    src, dst = iota((512, 256), 0) % PLANE, iota((512, 256), 1)
    gap = jnp.abs(src - dst)
    edge = (src % CY == 0) | (src % CY == CY - 1) | (dst % CY == 0) | (dst % CY == CY - 1)
    NN[...] = jnp.where(((gap == 1) | (gap == CY)) & ~edge, 1.0, 0.0).astype(BF)

    for copy in loads[:3]:
        copy.wait()
    turn = (slots - rot * CAP) % slots

    def turned(x):
        return jnp.where(m == 0, pltpu.roll(x, turn, axis=1), x)

    SB[...] = turned(SB[...])
    SC[...] = turned(SC[...])
    SF[...] = turned(SF[...])

    @pl.loop(0, tiles)
    def _(t):
        cols = pl.ds(pl.multiple_of(t * TILE, TILE), TILE)
        b = SB[:, cols]
        fz, fx, fy = SF[0:1, cols], SF[1:2, cols], SF[2:3, cols]
        z, x, y = b >> 8, (b >> 5) & 7, b & 31

        def hat(count, at, frac):
            i = iota((count, TILE), 0)
            return jnp.where(i == at, 1.0 - frac, jnp.where(i == at + 1, frac, 0.0))

        hx, hy = hat(CX, x, fx), hat(CY, y, fy)
        for i in range(CX):
            w = hx[i : i + 1] * hy
            hi = w.astype(BF)
            lo = (w - hi.astype(F32)).astype(BF)
            W3[i * CY : (i + 1) * CY, cols] = hi
            W3[PLANE + i * CY : PLANE + (i + 1) * CY, cols] = hi
            W3[2 * PLANE + i * CY : 2 * PLANE + (i + 1) * CY, cols] = lo
        WZ[:, cols] = hat(CZ, z, fz)
        c = SC[:, cols]
        ZO[:, cols] = jnp.where(iota((CZ, TILE), 0) == (c >> 8), 1.0, 0.0).astype(BF)
        cq = ((c >> 5) & 7) * 2 + jnp.where((c & 31) == 0, 0, 1)
        QO[:, cols] = jnp.where(iota((16, TILE), 0) == cq, 1.0, 0.0)

    def split(h, x):
        cols = pl.ds(h * LANES, LANES)
        hi = x.astype(BF)
        A3[:, pl.ds(h * LANES, LANES)] = hi
        A3[:, pl.ds(PLANE + h * LANES, LANES)] = (x - hi.astype(F32)).astype(BF)
        A3[:, pl.ds(2 * PLANE + h * LANES, LANES)] = hi

    lane1 = iota((CZ, LANES), 1)

    def pack(it, get):
        a = get(0, 0)
        z = get(1, 0)
        za = pltpu.roll(z, 32, axis=1)
        sl, sr = a, za
        for f in range(1, 4):
            here = (lane1 >= 32 * f) & (lane1 < 32 * f + 32)
            sl = jnp.where(here, pltpu.roll(get(0, f), 32 * f, axis=1), sl)
            sr = jnp.where(here, pltpu.roll(get(1, f), (32 * f + 32) % 128, axis=1), sr)
        sendH[it, 0] = sl
        sendH[it, 1] = sr

    loads[3].wait()
    pack(0, lambda h, f: F0[f * CZ : (f + 1) * CZ, h * LANES : (h + 1) * LANES])
    for h in range(2):
        split(h, F0[:, h * LANES : (h + 1) * LANES])

    pl.semaphore_wait(barrier, n + 4)

    for it in range(ITERS):
        halos = [
            pltpu.make_async_remote_copy(
                src_ref=sendH.at[it, e], dst_ref=recvH.at[it, e],
                send_sem=hs_sem.at[it, e], recv_sem=hr_sem.at[it, e],
                device_id=(m, left if e == 0 else right), device_id_type=MESH,
            )
            for e in range(2)
        ]
        for copy in halos:
            copy.start()

        def send(t):
            tile = lax.rem(t + d // 4, tiles)
            for i in range(4):
                peer = tile * 4 + i
                pltpu.make_async_remote_copy(
                    src_ref=sendS.at[it, tile * 2 + i // 2], dst_ref=recvS.at[it, d],
                    send_sem=s_sem.at[it], recv_sem=r_sem.at[it],
                    device_id=(1 - m, peer), device_id_type=MESH,
                ).start()

        @pl.loop(0, tiles)
        def _(t):
            tile = lax.rem(t + d // 4, tiles)
            cols = pl.ds(pl.multiple_of(tile * TILE, TILE), TILE)

            @pl.when(t > 0)
            def _():
                send(t - 1)

            p = jnp.dot(A3[...], W3[:, cols], preferred_element_type=F32)
            s = jnp.sum(p.reshape(4, CZ, TILE) * WZ[:, cols][None], axis=1)
            sendS[it, tile * 2] = s[:, :LANES]
            sendS[it, tile * 2 + 1] = s[:, LANES:]

        send(tiles - 1)

        if it == 0:
            loads[4].wait()
            loads[5].wait()
            for h in range(2):
                lanes = slice(h * LANES, (h + 1) * LANES)
                inv = 1.0 / SV[:, lanes]
                for f in range(4):
                    k = f // 3
                    rows = slice(h * 512 + f * CZ, h * 512 + (f + 1) * CZ)
                    c = KV[k * CZ : (k + 1) * CZ, lanes]
                    EP[rows] = (1.0 + 4.0 * c) * inv
                    CS[rows] = c * inv
                    IN[rows] = F0[f * CZ : (f + 1) * CZ, lanes] * inv

            def factor(zz, hprev):
                for u in range(8):
                    z = zz * 8 + u
                    t = EP[pl.ds(z, 8, stride=CZ)] + hprev
                    g = 1.0 / (1.0 + t)
                    G[pl.ds(z, 8, stride=CZ)] = g
                    hprev = t * g
                return hprev

            lax.fori_loop(0, CZ // 8, factor, jnp.ones((8, LANES), F32))

        NS[...] = jnp.dot(A3[:, : 2 * PLANE], NN[...], preferred_element_type=F32)
        for copy in halos:
            copy.wait()
        hr, hl = recvH[it, 0], recvH[it, 1]
        for h in range(2):
            for f in range(4):
                rows = slice(h * 512 + f * CZ, h * 512 + (f + 1) * CZ)
                x = NS[f * CZ : (f + 1) * CZ, h * LANES : (h + 1) * LANES]
                if h == 0:
                    x = x + jnp.where(lane1 < 32, pltpu.roll(hl, (128 - 32 * f) % 128, axis=1), 0.0)
                else:
                    x = x + jnp.where(lane1 >= 96, pltpu.roll(hr, 96 - 32 * f, axis=1), 0.0)
                R[rows] = IN[rows] + CS[rows] * x

        every = pltpu.make_async_copy(recvS.at[it], recvS.at[it], r_sem.at[it])
        every.wait()
        low = iota((n // 2, 4, LANES), 2) < CAP
        got = recvS[it].reshape(n // 2, 2, 4, LANES)
        even, odd = got[:, 0], got[:, 1]
        first = lax.rem(d, 2) == 0
        v = jnp.where(
            low,
            jnp.where(first, even, pltpu.roll(even, CAP, axis=2)),
            jnp.where(first, pltpu.roll(odd, CAP, axis=2), odd),
        )
        for i in range(n // 2):
            V2[:, i * LANES : (i + 1) * LANES] = v[i]
        rest = V2[...]
        for piece in range(3):
            part = rest.astype(BF).astype(F32)
            rest = rest - part
            for f in range(4):
                QV[piece * 64 + f * 16 : piece * 64 + f * 16 + 16, :] = (QO[...] * part[f : f + 1]).astype(BF)
        dp = lax.dot_general(ZO[...], QV[...], (((1,), (1,)), ((), ())), preferred_element_type=F32).astype(BF)
        for h in range(2):
            fr = jnp.dot(dp, E[:, h * 512 : (h + 1) * 512], preferred_element_type=F32)
            nb = jnp.dot(dp, E[:, 1024 + h * 512 : 1024 + (h + 1) * 512], preferred_element_type=F32)
            for f in range(4):
                rows = slice(h * 512 + f * CZ, h * 512 + (f + 1) * CZ)
                FR[rows] = fr[:, f * LANES : (f + 1) * LANES]
                R[rows] = R[rows] + CS[rows] * nb[:, f * LANES : (f + 1) * LANES]

        def forward(zz, v):
            for u in range(8):
                at = pl.ds(zz * 8 + u, 8, stride=CZ)
                v = (R[at] + v) * G[at]
                D[at] = v
            return v

        lax.fori_loop(0, CZ // 8, forward, jnp.zeros((8, LANES), F32))

        def backward(zz, v):
            for u in range(8):
                at = pl.ds(CZ - 1 - (zz * 8 + u), 8, stride=CZ)
                v = D[at] + G[at] * v
                D[at] = v
            return v

        lax.fori_loop(0, CZ // 8, backward, jnp.zeros((8, LANES), F32))

        sent = pltpu.make_async_copy(recvS.at[it], recvS.at[it], s_sem.at[it])
        sent.wait()

        lane4 = iota((512, LANES), 1) % CY
        fringe = (lane4 == 0) | (lane4 == CY - 1)
        new = [jnp.where(fringe, FR[h * 512 : (h + 1) * 512], D[h * 512 : (h + 1) * 512]) for h in range(2)]
        if it < ITERS - 1:
            pack(it + 1, lambda h, f: new[h][f * CZ : (f + 1) * CZ])
            for h in range(2):
                split(h, new[h])
        else:
            for h in range(2):
                OUT[:, h * LANES : (h + 1) * LANES] = new[h]

    @pl.when(m == 0)
    def _():
        copy = pltpu.make_async_copy(OUT, out, o_sem)
        copy.start()
        copy.wait()

    @pl.when(m == 1)
    def _():
        copy = pltpu.make_async_remote_copy(
            src_ref=OUT, dst_ref=out, send_sem=m_sem.at[0], recv_sem=m_sem.at[1],
            device_id=(m, ahead), device_id_type=MESH,
        )
        copy.start()
        copy.wait()


def step(rot, n, args):
    slots = n * CAP
    vm = pltpu.VMEM
    return pl.pallas_call(
        functools.partial(kernel, rot, n),
        out_shape=jax.ShapeDtypeStruct((4 * CZ, PLANE), F32),
        in_specs=[pl.BlockSpec(memory_space=pl.ANY)] * 6,
        out_specs=pl.BlockSpec(memory_space=pl.ANY),
        scratch_shapes=[
            vm((512, 256), F32), vm((256, 256), F32), vm((128, 256), F32),
            vm((1, slots), jnp.int32), vm((3, slots), F32), vm((1, slots), jnp.int32),
            vm((512, 768), BF), vm((768, slots), BF), vm((CZ, slots), F32), vm((CZ, slots), BF),
            vm((16, slots), F32), vm((192, slots), BF), vm((192, 2048), BF), vm((512, 256), BF),
            vm((4, slots), F32),
            vm((1024, LANES), F32), vm((1024, LANES), F32), vm((1024, LANES), F32), vm((1024, LANES), F32),
            vm((1024, LANES), F32), vm((1024, LANES), F32), vm((1024, LANES), F32),
            vm((512, 256), F32), vm((512, 256), F32),
            vm((ITERS, n // 2, 4, LANES), F32), vm((ITERS, n, 4, LANES), F32),
            vm((ITERS, 2, CZ, LANES), F32), vm((ITERS, 2, CZ, LANES), F32),
            pltpu.SemaphoreType.DMA((6,)), pltpu.SemaphoreType.DMA((ITERS,)), pltpu.SemaphoreType.DMA((ITERS,)),
            pltpu.SemaphoreType.DMA((ITERS, 2)), pltpu.SemaphoreType.DMA((ITERS, 2)),
            pltpu.SemaphoreType.DMA((2,)), pltpu.SemaphoreType.DMA,
        ],
        compiler_params=pltpu.CompilerParams(collective_id=rot, has_side_effects=True),
        name=f"rotor_step_{rot}",
    )(*args)


def solution(mesh):
    n = mesh.shape["blk"]

    def local(rotation_step, field_state, diffusivity, stretch, donor_base, donor_frac, fringe_cell):
        slots = n * CAP
        args = (
            field_state.reshape(4 * CZ, PLANE),
            diffusivity.reshape(2 * CZ, PLANE),
            stretch.reshape(CZ, PLANE),
            donor_base.reshape(1, slots),
            donor_frac.reshape(3, slots),
            fringe_cell.reshape(1, slots),
        )
        branches = [functools.partial(lambda rot, a: step(rot, n, a), rot) for rot in range(1, TURN_MOST + 1)]
        new = lax.switch(jnp.clip(rotation_step[0] - 1, 0, TURN_MOST - 1), branches, args)
        return new.reshape(1, 1, 4, CZ, PLANE)

    placed = (
        P(),
        P("mesh", "blk", None, None, None),
        P("mesh", "blk", None, None, None),
        P("mesh", "blk", None, None),
        P("mesh", "blk", None),
        P("mesh", "blk", None, None),
        P("mesh", "blk", None),
    )
    return jax.shard_map(
        local, mesh=mesh, in_specs=placed,
        out_specs=P("mesh", "blk", None, None, None), check_vma=False,
    )
```

```python
import functools

import jax
import jax.numpy as jnp
from jax import lax
from jax.experimental import pallas as pl
from jax.experimental.pallas import tpu as pltpu
from jax.sharding import PartitionSpec as P

CX, CY, CZ = 8, 32, 128
PLANE = CX * CY
ITERS = 2
TURN_MOST = 7
CAP = 64
TILE = 1024
LANES = 128
PITCH = 132
MESH = pl.DeviceIdType.MESH
BF = jnp.bfloat16
F32 = jnp.float32


def iota(shape, dim):
    return lax.broadcasted_iota(jnp.int32, shape, dim)


def kernel(
    rot, n,
    fs, kap, st, db, df, fc, out,
    F0, KV, SV, SB, SF, SC, A3, WH, WL, WZ, ZO, QO, QV, E, NN, V2,
    EP, CS, IN, R, G, D, V, FR, NS, EARLY, GOT, LATE,
    sendS, recvS, sendH, recvH,
    in_sem, s_sem, r_sem, hs_sem, hr_sem, m_sem,
):
    m = lax.axis_index("mesh")
    d = lax.axis_index("blk")
    slots = n * CAP
    tiles = slots // TILE
    right, left = lax.rem(d + 1, n), lax.rem(d + n - 1, n)
    ahead, back = lax.rem(d + rot, n), lax.rem(d + n - rot, n)

    loads = [
        pltpu.make_async_copy(src, dst, in_sem.at[i])
        for i, (src, dst) in enumerate(((db, SB), (df, SF), (fc, SC), (fs, F0), (kap, KV), (st, SV)))
    ]
    for copy in loads:
        copy.start()

    barrier = pltpu.get_barrier_semaphore()
    for peer in (left, right, ahead, back):
        pl.semaphore_signal(barrier, inc=1, device_id=(m, peer), device_id_type=MESH)

    @pl.loop(0, n // 16)
    def _(i):
        for u in range(16):
            peer = lax.rem(d + i * 16 + u, n)
            pl.semaphore_signal(barrier, inc=1, device_id=(1 - m, peer), device_id_type=MESH)

    row, col = iota((128, 2 * 2 * 4 * LANES), 0), iota((128, 2 * 2 * 4 * LANES), 1)
    q = row & 15
    kind, half, fld, lane = col >> 10, (col >> 9) & 1, (col >> 7) & 3, col & 127
    place = (q >> 1) * CY + (q & 1) * (CY - 1) + kind * (1 - 2 * (q & 1))
    E[...] = jnp.where((((row >> 4) & 3) == fld) & (half * LANES + lane == place), 1.0, 0.0).astype(BF)
    src, dst = iota((512, 256), 0) & 255, iota((512, 256), 1)
    gap = jnp.abs(src - dst)
    sy, dy = src & 31, dst & 31
    edge = (sy == 0) | (sy == CY - 1) | (dy == 0) | (dy == CY - 1)
    NN[...] = jnp.where(((gap == 1) | (gap == CY)) & ~edge, 1.0, 0.0).astype(BF)

    for copy in loads[:3]:
        copy.wait()
    turn = (slots - rot * CAP) % slots

    def turned(ref, i):
        x = ref[:, i * slots : (i + 1) * slots]
        return jnp.where(m == 0, pltpu.roll(x, turn, axis=1), x)

    for ref, count in ((SB, 1), (SC, 1), (SF, 3)):
        for i in range(count):
            ref[:, i * slots : (i + 1) * slots] = turned(ref, i)

    @pl.loop(0, slots // 256)
    def _(t):
        cols = pl.ds(pl.multiple_of(t * 256, 256), 256)
        b = SB[:, cols]
        fz, fx, fy = (SF[:, pl.ds(pl.multiple_of(i * slots + t * 256, 256), 256)] for i in range(3))
        z, x, y = b >> 8, (b >> 5) & 7, b & 31

        def hat(count, at, frac):
            i = iota((count, 256), 0)
            return jnp.where(i == at, 1.0 - frac, jnp.where(i == at + 1, frac, 0.0))

        hx, hy = hat(CX, x, fx), hat(CY, y, fy)
        for i in range(CX):
            w = hx[i : i + 1] * hy
            hi = w.astype(BF)
            WH[i * CY : (i + 1) * CY, cols] = hi
            WL[i * CY : (i + 1) * CY, cols] = (w - hi.astype(F32)).astype(BF)
        WZ[:, cols] = hat(CZ, z, fz)
        c = SC[:, cols]
        ZO[:, cols] = jnp.where(iota((CZ, 256), 0) == (c >> 8), 1.0, 0.0).astype(BF)
        cq = ((c >> 5) & 7) * 2 + jnp.where((c & 31) == 0, 0, 1)
        QO[:, cols] = jnp.where(iota((16, 256), 0) == cq, 1.0, 0.0)

    def split(h, x):
        hi = x.astype(BF)
        A3[:, h * LANES : (h + 1) * LANES] = hi
        A3[:, PLANE + h * LANES : PLANE + (h + 1) * LANES] = (x - hi.astype(F32)).astype(BF)
        A3[:, 2 * PLANE + h * LANES : 2 * PLANE + (h + 1) * LANES] = hi

    lane1 = iota((CZ, LANES), 1)

    def pack(it, get):
        sl, sr = get(0, 0), pltpu.roll(get(1, 0), 32, axis=1)
        for f in range(1, 4):
            here = (lane1 >> 5) == f
            sl = jnp.where(here, pltpu.roll(get(0, f), 32 * f, axis=1), sl)
            sr = jnp.where(here, pltpu.roll(get(1, f), (32 * f + 32) % 128, axis=1), sr)
        sendH[it, 0] = sl
        sendH[it, 1] = sr

    y4 = lane1 & 31
    fringe = (y4 == 0) | (y4 == CY - 1)

    def new(h, f):
        return jnp.where(fringe, FR[rows_of(h, f)], V[rows_of(h, f)])

    def rows_of(h, f):
        return slice((h * 4 + f) * PITCH, (h * 4 + f) * PITCH + CZ)

    def at(z):
        return pl.ds(z, 8, stride=PITCH)

    top, low = CZ // 2 - 1, CZ // 2

    def solve():
        def forward(i, carry):
            a, b = carry
            for u in range(8):
                z = i * 8 + u
                a = (R[at(z)] + a) * G[at(z)]
                b = (R[at(CZ - 1 - z)] + b) * G[at(CZ - 1 - z)]
                D[at(z)] = a
                D[at(CZ - 1 - z)] = b
            return a, b

        zero = jnp.zeros((8, LANES), F32)
        a, b = lax.fori_loop(0, CZ // 16, forward, (zero, zero))
        a = (a + G[at(top)] * b) * LATE[CZ : CZ + 8]
        b = b + G[at(low)] * a
        V[at(top)] = a
        V[at(low)] = b

        def backward(i, carry):
            a, b = carry
            for u in range(9):
                z = i * 9 + u + 1
                a = D[at(top - z)] + G[at(top - z)] * a
                b = D[at(low + z)] + G[at(low + z)] * b
                V[at(top - z)] = a
                V[at(low + z)] = b
            return a, b

        lax.fori_loop(0, 7, backward, (a, b))

    loads[3].wait()
    pack(0, lambda h, f: F0[f * CZ : (f + 1) * CZ, h * LANES : (h + 1) * LANES])
    for h in range(2):
        split(h, F0[:, h * LANES : (h + 1) * LANES])

    pl.semaphore_wait(barrier, n + 4)

    early = pltpu.make_async_remote_copy(
        src_ref=EARLY, dst_ref=GOT, send_sem=m_sem.at[0], recv_sem=m_sem.at[1],
        device_id=(m, ahead), device_id_type=MESH,
    )
    late = pltpu.make_async_remote_copy(
        src_ref=LATE.at[pl.ds(0, CZ)], dst_ref=LATE.at[pl.ds(CZ + 8, CZ)], send_sem=m_sem.at[2], recv_sem=m_sem.at[3],
        device_id=(m, ahead), device_id_type=MESH,
    )

    @pl.loop(0, ITERS)
    def _(it):
        halos = [
            pltpu.make_async_remote_copy(
                src_ref=sendH.at[it, e], dst_ref=recvH.at[it, e],
                send_sem=hs_sem.at[it, e], recv_sem=hr_sem.at[it, e],
                device_id=(m, left if e == 0 else right), device_id_type=MESH,
            )
            for e in range(2)
        ]
        for copy in halos:
            copy.start()

        per = TILE // CAP

        def send(t):
            tile = lax.rem(t + d // per, tiles)
            for i in range(per):
                pi = lax.rem(i + d, per)
                pltpu.make_async_remote_copy(
                    src_ref=sendS.at[it, i % 2, tile * (per // 2) + pi // 2], dst_ref=recvS.at[it, d],
                    send_sem=s_sem.at[it], recv_sem=r_sem.at[it],
                    device_id=(1 - m, tile * per + pi), device_id_type=MESH,
                ).start()

        @pl.loop(0, tiles)
        def _(t):
            tile = lax.rem(t + d // per, tiles)
            cols = pl.ds(pl.multiple_of(tile * TILE, TILE), TILE)

            @pl.when(t > 0)
            def _():
                send(t - 1)

            wh = WH[:, cols]
            p = jnp.dot(A3[...], jnp.concatenate([wh, wh, WL[:, cols]], axis=0), preferred_element_type=F32)
            s = jnp.sum(p.reshape(4, CZ, TILE) * WZ[:, cols][None], axis=1)
            for i in range(per // 2):
                x = s[:, i * LANES : (i + 1) * LANES]
                sendS[it, 0, tile * (per // 2) + i] = x
                sendS[it, 1, tile * (per // 2) + i] = pltpu.roll(x, CAP, axis=1)

        send(tiles - 1)

        @pl.when(it == 0)
        def _():
            loads[4].wait()
            loads[5].wait()
            for h in range(2):
                lanes = slice(h * LANES, (h + 1) * LANES)
                inv = 1.0 / SV[:, lanes]
                for f in range(4):
                    k = f // 3
                    c = KV[k * CZ : (k + 1) * CZ, lanes]
                    EP[rows_of(h, f)] = (1.0 + 4.0 * c) * inv
                    CS[rows_of(h, f)] = c * inv
                    IN[rows_of(h, f)] = F0[f * CZ : (f + 1) * CZ, lanes] * inv

            def factor(i, carry):
                ha, hb = carry
                for u in range(8):
                    z = i * 8 + u
                    ta, tb = EP[at(z)] + ha, EP[at(CZ - 1 - z)] + hb
                    ga, gb = 1.0 / (1.0 + ta), 1.0 / (1.0 + tb)
                    G[at(z)] = ga
                    G[at(CZ - 1 - z)] = gb
                    ha, hb = ta * ga, tb * gb
                return ha, hb

            one = jnp.ones((8, LANES), F32)
            ha, hb = lax.fori_loop(0, CZ // 16, factor, (one, one))
            LATE[CZ : CZ + 8] = 1.0 / (ha + hb - ha * hb)

        NS[...] = jnp.dot(A3[:, : 2 * PLANE], NN[...], preferred_element_type=F32)
        for copy in halos:
            copy.wait()
        hr, hl = recvH[it, 0], recvH[it, 1]
        for h in range(2):
            for f in range(4):
                x = NS[f * CZ : (f + 1) * CZ, h * LANES : (h + 1) * LANES]
                if h == 0:
                    x = x + jnp.where(lane1 < 32, pltpu.roll(hl, (128 - 32 * f) % 128, axis=1), 0.0)
                else:
                    x = x + jnp.where(lane1 >= 96, pltpu.roll(hr, 96 - 32 * f, axis=1), 0.0)
                R[rows_of(h, f)] = IN[rows_of(h, f)] + CS[rows_of(h, f)] * x

        @pl.when((it == ITERS - 1) & (m == 1))
        def _():
            solve()
            for h in range(2):
                for f in range(4):
                    EARLY[f * CZ : (f + 1) * CZ, h * LANES : (h + 1) * LANES] = V[rows_of(h, f)]
            early.start()

        pltpu.make_async_copy(recvS.at[it], recvS.at[it], r_sem.at[it]).wait()
        got = recvS[it].reshape(n // 2, 2, 4, LANES)
        v = jnp.where(iota((n // 2, 4, LANES), 2) < CAP, got[:, 0], got[:, 1])
        for i in range(n // 2):
            V2[:, i * LANES : (i + 1) * LANES] = v[i]
        rest = V2[...]
        for piece in range(2):
            part = rest.astype(BF).astype(F32)
            rest = rest - part
            for f in range(4):
                QV[piece * 64 + f * 16 : piece * 64 + f * 16 + 16, :] = (QO[...] * part[f : f + 1]).astype(BF)
        dp = lax.dot_general(ZO[...], QV[...], (((1,), (1,)), ((), ())), preferred_element_type=F32).astype(BF)
        for h in range(2):
            fr = jnp.dot(dp, E[:, h * 512 : (h + 1) * 512], preferred_element_type=F32)
            nb = jnp.dot(dp, E[:, 1024 + h * 512 : 1024 + (h + 1) * 512], preferred_element_type=F32)
            for f in range(4):
                FR[rows_of(h, f)] = fr[:, f * LANES : (f + 1) * LANES]
                R[rows_of(h, f)] = R[rows_of(h, f)] + CS[rows_of(h, f)] * nb[:, f * LANES : (f + 1) * LANES]
        solve()

        pltpu.make_async_copy(recvS.at[it], recvS.at[it], s_sem.at[it]).wait()

        @pl.when(it < ITERS - 1)
        def _():
            pack(it + 1, new)
            for h in range(2):
                split(h, jnp.concatenate([new(h, f) for f in range(4)], axis=0))

    @pl.when(m == 0)
    def _():
        for h in range(2):
            for f in range(4):
                out[f * CZ : (f + 1) * CZ, h * LANES : (h + 1) * LANES] = new(h, f)

    @pl.when(m == 1)
    def _():
        yy = lane1 & 3
        pick = ((lane1 >> 2) & 3) * CY + yy + jnp.where(yy >= 2, CY - 4, 0)
        acc = jnp.zeros((CZ, LANES), F32)
        for h in range(2):
            for f in range(4):
                x = jnp.take_along_axis(new(h, f), pick, axis=1, mode="promise_in_bounds")
                acc = jnp.where((lane1 >> 4) == f * 2 + h, x, acc)
        LATE[:CZ] = acc
        late.start()
        early.wait()
        late.wait()
        tail = LATE[CZ + 8 :]
        y = lane1 & 31
        home = (lane1 >> 5) * 4 + (y & 3)
        rim = (y < 2) | (y >= CY - 2)
        for h in range(2):
            for f in range(4):
                x = jnp.take_along_axis(tail, home + (f * 32 + h * 16), axis=1, mode="promise_in_bounds")
                block = (slice(f * CZ, (f + 1) * CZ), slice(h * LANES, (h + 1) * LANES))
                out[block] = jnp.where(rim, x, GOT[block])


def step(rot, n, args):
    slots = n * CAP
    vm = pltpu.VMEM
    dma = pltpu.SemaphoreType.DMA
    tall = vm((8 * PITCH, LANES), F32)
    return pl.pallas_call(
        functools.partial(kernel, rot, n),
        out_shape=jax.ShapeDtypeStruct((4 * CZ, PLANE), F32),
        in_specs=[pl.BlockSpec(memory_space=pl.ANY)] * 6,
        out_specs=pl.BlockSpec(memory_space=pltpu.VMEM),
        scratch_shapes=[
            vm((512, 256), F32), vm((256, 256), F32), vm((128, 256), F32),
            vm((1, slots), jnp.int32), vm((1, 3 * slots), F32), vm((1, slots), jnp.int32),
            vm((512, 768), BF), vm((256, slots), BF), vm((256, slots), BF), vm((CZ, slots), F32), vm((CZ, slots), BF),
            vm((16, slots), F32), vm((128, slots), BF), vm((128, 2048), BF), vm((512, 256), BF),
            vm((4, slots), F32),
            tall, tall, tall, tall, tall, tall, tall, tall,
            vm((512, 256), F32), vm((512, 256), F32), vm((512, 256), F32), vm((2 * CZ + 8, LANES), F32),
            vm((ITERS, 2, n // 2, 4, LANES), F32), vm((ITERS, n, 4, LANES), F32),
            vm((ITERS, 2, CZ, LANES), F32), vm((ITERS, 2, CZ, LANES), F32),
            dma((6,)), dma((ITERS,)), dma((ITERS,)), dma((ITERS, 2)), dma((ITERS, 2)), dma((4,)),
        ],
        compiler_params=pltpu.CompilerParams(collective_id=rot, has_side_effects=True),
        name=f"rotor_step_{rot}",
    )(*args)


def solution(mesh):
    n = mesh.shape["blk"]

    def local(rotation_step, field_state, diffusivity, stretch, donor_base, donor_frac, fringe_cell):
        slots = n * CAP
        args = (
            field_state.reshape(4 * CZ, PLANE),
            diffusivity.reshape(2 * CZ, PLANE),
            stretch.reshape(CZ, PLANE),
            donor_base.reshape(1, slots),
            donor_frac.reshape(1, 3 * slots),
            fringe_cell.reshape(1, slots),
        )
        branches = [functools.partial(lambda rot, a: step(rot, n, a), rot) for rot in range(1, TURN_MOST + 1)]
        new = lax.switch(jnp.clip(rotation_step[0] - 1, 0, TURN_MOST - 1), branches, args)
        return new.reshape(1, 1, 4, CZ, PLANE)

    placed = (
        P(),
        P("mesh", "blk", None, None, None),
        P("mesh", "blk", None, None, None),
        P("mesh", "blk", None, None),
        P("mesh", "blk", None),
        P("mesh", "blk", None, None),
        P("mesh", "blk", None),
    )
    return jax.shard_map(
        local, mesh=mesh, in_specs=placed,
        out_specs=P("mesh", "blk", None, None, None), check_vma=False,
    )
```

```python
import functools

import jax
import jax.numpy as jnp
from jax import lax
from jax.experimental import pallas as pl
from jax.experimental.pallas import tpu as pltpu
from jax.sharding import PartitionSpec as P

CX, CY, CZ = 8, 32, 128
PLANE = CX * CY
ITERS = 2
TURN_MOST = 7
CAP = 64
TILE = 1024
SIDE = 4
GROUPS = sorted(
    ((dy, dx) for dy in range(SIDE) for dx in range(SIDE)),
    key=lambda o: -sum(min(a, SIDE - a) for a in o),
)
ALONG_Z = (2, 1, 3, 0)
OPEN = 2
GROUP = SIDE * CAP


def packed(values):
    word = sum(v << (2 * i) for i, v in enumerate(values))
    return word - (1 << 32) if word >= 1 << 31 else word

LANES = 128
PITCH = 132
MESH = pl.DeviceIdType.MESH
BF = jnp.bfloat16
F32 = jnp.float32


def iota(shape, dim):
    return lax.broadcasted_iota(jnp.int32, shape, dim)


def kernel(
    rot, n,
    fs, kap, st, db, df, fc, out,
    F0, KV, SV, SB, SF, SC, A3, WH, WL, WZ, ZO, QO, QV, E, NN, V2,
    EP, CS, IN, R, G, D, V, FR, NS, VE, GOT, MID,
    sendS, recvS, sendH, recvH,
    in_sem, s_sem, r_sem, hs_sem, hr_sem, m_sem,
):
    m = lax.axis_index("mesh")
    d = lax.axis_index("blk")
    slots = n * CAP
    tiles = slots // TILE
    moved = m == 1

    def near(delta):
        return (d + delta) & (n - 1)

    loads = [
        pltpu.make_async_copy(src, dst, in_sem.at[i])
        for i, (src, dst) in enumerate(
            ((db, SB), (df, SF), (fc, SC.at[0]), (fs, F0), (kap, KV.at[0]), (st, SV.at[0]))
        )
    ]
    for copy in loads:
        copy.start()

    py = [(((d >> 4) + o) & 3) << 4 for o in range(SIDE)]
    px = [(((d >> 2) + o) & 3) << 2 for o in range(SIDE)]
    pz = [(d + o) & 3 for o in range(SIDE)]
    barrier = pltpu.get_barrier_semaphore()
    for dy, dx in GROUPS:
        for dz in ALONG_Z:
            pl.semaphore_signal(barrier, inc=1, device_id=(1 - m, py[dy] + px[dx] + pz[dz]), device_id_type=MESH)
    deltas = sorted({s * k for s in (1, -1) for k in (1, rot, rot + 1, rot - 1) if k})
    for delta in deltas:
        pl.semaphore_signal(barrier, inc=1, device_id=(m, near(delta)), device_id_type=MESH)

    for copy in loads[:3]:
        copy.wait()
    turn = (slots - rot * CAP) % slots

    def turned(x):
        return jnp.where(m == 0, pltpu.roll(x, turn, axis=1), x)

    SB[...] = turned(SB[...])
    SC[0] = turned(SC[0])
    for i in range(3):
        SF[:, i * slots : (i + 1) * slots] = turned(SF[:, i * slots : (i + 1) * slots])

    def hat(count, at, frac):
        i = iota((count, GROUP), 0)
        return jnp.where(i == at, 1.0 - frac, jnp.where(i == at + 1, frac, 0.0))

    def weigh(g):
        cols = pl.ds(pl.multiple_of(g * GROUP, GROUP), GROUP)
        b = SB[:, cols]
        fz, fx, fy = (SF[:, pl.ds(pl.multiple_of(i * slots + g * GROUP, GROUP), GROUP)] for i in range(3))
        hx, hy = hat(CX, (b >> 5) & 7, fx), hat(CY, b & 31, fy)
        for i in range(CX):
            w = hx[i : i + 1] * hy
            hi = w.astype(BF)
            WH[i * CY : (i + 1) * CY, cols] = hi
            WL[i * CY : (i + 1) * CY, cols] = (w - hi.astype(F32)).astype(BF)
        WZ[:, cols] = hat(CZ, b >> 8, fz)

    def split(h, x):
        hi = x.astype(BF)
        A3[:, h * LANES : (h + 1) * LANES] = hi
        A3[:, PLANE + h * LANES : PLANE + (h + 1) * LANES] = (x - hi.astype(F32)).astype(BF)
        A3[:, 2 * PLANE + h * LANES : 2 * PLANE + (h + 1) * LANES] = hi

    lane1 = iota((CZ, LANES), 1)
    y4 = lane1 & 31
    fringe = (y4 == 0) | (y4 == CY - 1)

    def pack(it, get):
        sl, sr = get(0, 0), pltpu.roll(get(1, 0), 32, axis=1)
        for f in range(1, 4):
            here = (lane1 >> 5) == f
            sl = jnp.where(here, pltpu.roll(get(0, f), 32 * f, axis=1), sl)
            sr = jnp.where(here, pltpu.roll(get(1, f), (32 * f + 32) % 128, axis=1), sr)
        sendH[it, 0] = sl
        sendH[it, 1] = sr

    def rows_of(h, f):
        return slice((h * 4 + f) * PITCH, (h * 4 + f) * PITCH + CZ)

    BLOCKS = [(h, f) for h in range(2) for f in range(4)]

    def at(z):
        return pl.ds(z, 8, stride=PITCH)

    top, low = CZ // 2 - 1, CZ // 2

    def solve(V):
        def forward(i, carry):
            a, b = carry
            for u in range(8):
                z = i * 8 + u
                a = (R[at(z)] + a) * G[at(z)]
                b = (R[at(CZ - 1 - z)] + b) * G[at(CZ - 1 - z)]
                D[at(z)] = a
                D[at(CZ - 1 - z)] = b
            return a, b

        zero = jnp.zeros((8, LANES), F32)
        a, b = lax.fori_loop(0, CZ // 16, forward, (zero, zero))
        a = (a + G[at(top)] * b) * MID[...]
        b = b + G[at(low)] * a
        V[at(top)] = a
        V[at(low)] = b

        def backward(i, carry):
            a, b = carry
            for u in range(9):
                z = i * 9 + u + 1
                a = D[at(top - z)] + G[at(top - z)] * a
                b = D[at(low + z)] + G[at(low + z)] * b
                V[at(top - z)] = a
                V[at(low + z)] = b
            return a, b

        lax.fori_loop(0, 7, backward, (a, b))

    def from_within():
        NS[...] = jnp.dot(A3[:, : 2 * PLANE], NN[...], preferred_element_type=F32)
        for h, f in BLOCKS:
            x = NS[f * CZ : (f + 1) * CZ, h * LANES : (h + 1) * LANES]
            R[rows_of(h, f)] = IN[rows_of(h, f)] + CS[rows_of(h, f)] * x

    loads[3].wait()
    pack(0, lambda h, f: F0[f * CZ : (f + 1) * CZ, h * LANES : (h + 1) * LANES])
    for h in range(2):
        split(h, F0[:, h * LANES : (h + 1) * LANES])

    early = pltpu.make_async_remote_copy(
        src_ref=VE, dst_ref=GOT, send_sem=m_sem.at[0], recv_sem=m_sem.at[1],
        device_id=(m, near(rot)), device_id_type=MESH,
    )
    stay = pltpu.make_async_copy(VE, GOT, m_sem.at[2])
    carried = [
        pltpu.make_async_remote_copy(
            src_ref=ref.at[0], dst_ref=ref.at[1], send_sem=m_sem.at[3 + 2 * i], recv_sem=m_sem.at[4 + 2 * i],
            device_id=(m, near(rot)), device_id_type=MESH,
        )
        for i, ref in enumerate((KV, SV, SC))
    ]

    @pl.loop(0, ITERS)
    def _(it):
        ahead = (it > 0) & moved
        edge = [(sendH.at[it, e], recvH.at[it, e]) for e in range(2)]

        def halo(e, delta):
            return pltpu.make_async_remote_copy(
                src_ref=edge[e][0], dst_ref=edge[e][1],
                send_sem=hs_sem.at[it, e], recv_sem=hr_sem.at[it, e],
                device_id=(m, near(delta)), device_id_type=MESH,
            )

        @pl.when(it > 0)
        def _():
            from_within()
            for k in range(8):
                VE[k * PITCH + CZ : (k + 1) * PITCH] = jnp.zeros((PITCH - CZ, LANES), F32)
            solve(VE)
            R[...] = jnp.zeros_like(R)

        def group(k):
            dy, dx = (packed([g[0] for g in GROUPS]) >> (2 * k)) & 3, (packed([g[1] for g in GROUPS]) >> (2 * k)) & 3
            return ((((d >> 4) + dy) & 3) << 2) + (((d >> 2) + dx) & 3)

        per = TILE // GROUP
        shift = jnp.where((it > 0) & (m == 0), rot, 0)

        def send(t):
            for j in range(per):
                g = group(t * per + j)
                for dz in ALONG_Z:
                    pltpu.make_async_remote_copy(
                        src_ref=sendS.at[it, dz % 2, g * 2 + (pz[dz] >> 1)], dst_ref=recvS.at[it, d],
                        send_sem=s_sem.at[it], recv_sem=r_sem.at[it],
                        device_id=(1 - m, (g * SIDE + pz[dz] + shift) & (n - 1)), device_id_type=MESH,
                    ).start()

        @pl.loop(0, tiles)
        def _(t):
            @pl.when((it == 0) & (t == OPEN))
            def _():
                pl.semaphore_wait(barrier, n + len(deltas))

                @pl.loop(0, OPEN - 1)
                def _(u):
                    send(u)

            begin = t == jnp.where(it == 0, OPEN, 0)

            @pl.when(begin & jnp.logical_not(ahead))
            def _():
                halo(0, -1).start()
                halo(1, 1).start()

            @pl.when(begin & ahead)
            def _():
                if rot == 1:
                    pltpu.make_async_copy(edge[0][0], edge[0][1], hr_sem.at[it, 0]).start()
                else:
                    halo(0, rot - 1).start()
                halo(1, rot + 1).start()

            @pl.when(begin & (it > 0) & (m == 0))
            def _():
                stay.start()

            @pl.when(((it > 0) & (t > 0)) | (t >= OPEN))
            def _():
                send(t - 1)

            @pl.when(ahead)
            def _():
                for u in range(2):
                    rows = pl.ds((t * 2 + u) * PITCH, PITCH)
                    pltpu.make_async_remote_copy(
                        src_ref=VE.at[rows], dst_ref=GOT.at[rows], send_sem=m_sem.at[0], recv_sem=m_sem.at[1],
                        device_id=(m, near(rot)), device_id_type=MESH,
                    ).start()

            @pl.when(it == 0)
            def _():
                @pl.loop(0, per)
                def _(j):
                    weigh(group(t * per + j))

            cols = [pl.ds(pl.multiple_of(group(t * per + j) * GROUP, GROUP), GROUP) for j in range(per)]

            def gathered(ref):
                return jnp.concatenate([ref[:, c] for c in cols], axis=1)

            wh = gathered(WH)
            p = jnp.dot(A3[...], jnp.concatenate([wh, wh, gathered(WL)], axis=0), preferred_element_type=F32)
            s = jnp.sum(p.reshape(4, CZ, TILE) * gathered(WZ)[None], axis=1)
            for j in range(per):
                g = group(t * per + j)
                for i in range(2):
                    x = s[:, j * GROUP + i * LANES : j * GROUP + (i + 1) * LANES]
                    sendS[it, 0, g * 2 + i] = x
                    sendS[it, 1, g * 2 + i] = pltpu.roll(x, CAP, axis=1)

        send(tiles - 1)

        @pl.when(it == 0)
        def _():
            loads[4].wait()
            loads[5].wait()

        @pl.when((it == 0) & moved)
        def _():
            for copy in carried:
                copy.start()

        @pl.when(it == 0)
        def _():
            row, col = iota((128, 2 * 2 * 4 * LANES), 0), iota((128, 2 * 2 * 4 * LANES), 1)
            q = row & 15
            kind, half, fld, lane = col >> 10, (col >> 9) & 1, (col >> 7) & 3, col & 127
            place = (q >> 1) * CY + (q & 1) * (CY - 1) + kind * (1 - 2 * (q & 1))
            E[...] = jnp.where((((row >> 4) & 3) == fld) & (half * LANES + lane == place), 1.0, 0.0).astype(BF)
            src, dst = iota((512, 256), 0) & 255, iota((512, 256), 1)
            gap = jnp.abs(src - dst)
            sy, dy = src & 31, dst & 31
            rim = (sy == 0) | (sy == CY - 1) | (dy == 0) | (dy == CY - 1)
            NN[...] = jnp.where(((gap == 1) | (gap == CY)) & ~rim, 1.0, 0.0).astype(BF)

        @pl.when(ahead)
        def _():
            for copy in carried:
                copy.wait()

        @pl.when((it == 0) | moved)
        def _():
            @pl.loop(0, n // SIDE)
            def _(g):
                cols = pl.ds(pl.multiple_of(g * GROUP, GROUP), GROUP)
                c = SC[it, :, cols]
                ZO[:, cols] = jnp.where(iota((CZ, GROUP), 0) == (c >> 8), 1.0, 0.0).astype(BF)
                cq = ((c >> 5) & 7) * 2 + jnp.where((c & 31) == 0, 0, 1)
                QO[:, cols] = jnp.where(iota((16, GROUP), 0) == cq, 1.0, 0.0)

            for h in range(2):
                lanes = slice(h * LANES, (h + 1) * LANES)
                inv = 1.0 / SV[it, :, lanes]
                for f in range(4):
                    k = f // 3
                    c = KV[it, k * CZ : (k + 1) * CZ, lanes]
                    EP[rows_of(h, f)] = (1.0 + 4.0 * c) * inv
                    CS[rows_of(h, f)] = c * inv
                    IN[rows_of(h, f)] = F0[f * CZ : (f + 1) * CZ, lanes] * inv

            def factor(i, carry):
                ha, hb = carry
                for u in range(8):
                    z = i * 8 + u
                    ta, tb = EP[at(z)] + ha, EP[at(CZ - 1 - z)] + hb
                    ga, gb = 1.0 / (1.0 + ta), 1.0 / (1.0 + tb)
                    G[at(z)] = ga
                    G[at(CZ - 1 - z)] = gb
                    ha, hb = ta * ga, tb * gb
                return ha, hb

            one = jnp.ones((8, LANES), F32)
            ha, hb = lax.fori_loop(0, CZ // 16, factor, (one, one))
            MID[...] = 1.0 / (ha + hb - ha * hb)

        @pl.when(it == 0)
        def _():
            from_within()

        for e in range(2):
            halo(e, 1).wait_recv()
        halo(1, 1).wait_send()
        if rot == 1:

            @pl.when(jnp.logical_not(ahead))
            def _():
                halo(0, 1).wait_send()
        else:
            halo(0, 1).wait_send()
        hr, hl = recvH[it, 0], recvH[it, 1]
        for h, f in BLOCKS:
            if h == 0:
                x = jnp.where(lane1 < 32, pltpu.roll(hl, (128 - 32 * f) % 128, axis=1), 0.0)
            else:
                x = jnp.where(lane1 >= 96, pltpu.roll(hr, 96 - 32 * f, axis=1), 0.0)
            R[rows_of(h, f)] = R[rows_of(h, f)] + CS[rows_of(h, f)] * x

        pltpu.make_async_copy(recvS.at[it], recvS.at[it], r_sem.at[it]).wait()
        got = recvS[it].reshape(n // 2, 2, 4, LANES)
        v = jnp.where(iota((n // 2, 4, LANES), 2) < CAP, got[:, 0], got[:, 1])
        for i in range(n // 2):
            V2[:, i * LANES : (i + 1) * LANES] = v[i]
        rest = V2[...]
        for piece in range(2):
            part = rest.astype(BF).astype(F32)
            rest = rest - part
            for f in range(4):
                QV[piece * 64 + f * 16 : piece * 64 + f * 16 + 16, :] = (QO[...] * part[f : f + 1]).astype(BF)
        dp = lax.dot_general(ZO[...], QV[...], (((1,), (1,)), ((), ())), preferred_element_type=F32).astype(BF)
        for h in range(2):
            fr = jnp.dot(dp, E[:, h * 512 : (h + 1) * 512], preferred_element_type=F32)
            nb = jnp.dot(dp, E[:, 1024 + h * 512 : 1024 + (h + 1) * 512], preferred_element_type=F32)
            for f in range(4):
                FR[rows_of(h, f)] = fr[:, f * LANES : (f + 1) * LANES]
                R[rows_of(h, f)] = R[rows_of(h, f)] + CS[rows_of(h, f)] * nb[:, f * LANES : (f + 1) * LANES]
        solve(V)

        pltpu.make_async_copy(recvS.at[it], recvS.at[it], s_sem.at[it]).wait()

        @pl.when(it < ITERS - 1)
        def _():
            def new(h, f):
                return jnp.where(fringe, FR[rows_of(h, f)], V[rows_of(h, f)])

            pack(it + 1, new)
            for h in range(2):
                split(h, jnp.concatenate([new(h, f) for f in range(4)], axis=0))

    @pl.when(m == 0)
    def _():
        stay.wait()

    @pl.when(moved)
    def _():
        early.wait()

    for h, f in BLOCKS:
        out[f * CZ : (f + 1) * CZ, h * LANES : (h + 1) * LANES] = jnp.where(
            fringe, FR[rows_of(h, f)], V[rows_of(h, f)] + GOT[rows_of(h, f)]
        )


def step(rot, n, args):
    slots = n * CAP
    vm = pltpu.VMEM
    dma = pltpu.SemaphoreType.DMA
    tall = vm((8 * PITCH, LANES), F32)
    return pl.pallas_call(
        functools.partial(kernel, rot, n),
        out_shape=jax.ShapeDtypeStruct((4 * CZ, PLANE), F32),
        in_specs=[pl.BlockSpec(memory_space=pl.ANY)] * 6,
        out_specs=pl.BlockSpec(memory_space=pltpu.VMEM),
        scratch_shapes=[
            vm((512, 256), F32), vm((2, 256, 256), F32), vm((2, 128, 256), F32),
            vm((1, slots), jnp.int32), vm((1, 3 * slots), F32), vm((2, 1, slots), jnp.int32),
            vm((512, 768), BF), vm((256, slots), BF), vm((256, slots), BF), vm((CZ, slots), F32), vm((CZ, slots), BF),
            vm((16, slots), F32), vm((128, slots), BF), vm((128, 2048), BF), vm((512, 256), BF),
            vm((4, slots), F32),
            tall, tall, tall, tall, tall, tall, tall, tall,
            vm((512, 256), F32), tall, tall, vm((8, LANES), F32),
            vm((ITERS, 2, n // 2, 4, LANES), F32), vm((ITERS, n, 4, LANES), F32),
            vm((ITERS, 2, CZ, LANES), F32), vm((ITERS, 2, CZ, LANES), F32),
            dma((6,)), dma((ITERS,)), dma((ITERS,)), dma((ITERS, 2)), dma((ITERS, 2)), dma((9,)),
        ],
        compiler_params=pltpu.CompilerParams(collective_id=rot, has_side_effects=True),
        name=f"rotor_step_{rot}",
    )(*args)


def solution(mesh):
    n = mesh.shape["blk"]

    def local(rotation_step, field_state, diffusivity, stretch, donor_base, donor_frac, fringe_cell):
        slots = n * CAP
        args = (
            field_state.reshape(4 * CZ, PLANE),
            diffusivity.reshape(2 * CZ, PLANE),
            stretch.reshape(CZ, PLANE),
            donor_base.reshape(1, slots),
            donor_frac.reshape(1, 3 * slots),
            fringe_cell.reshape(1, slots),
        )
        branches = [functools.partial(lambda rot, a: step(rot, n, a), rot) for rot in range(1, TURN_MOST + 1)]
        new = lax.switch(jnp.clip(rotation_step[0] - 1, 0, TURN_MOST - 1), branches, args)
        return new.reshape(1, 1, 4, CZ, PLANE)

    placed = (
        P(),
        P("mesh", "blk", None, None, None),
        P("mesh", "blk", None, None, None),
        P("mesh", "blk", None, None),
        P("mesh", "blk", None),
        P("mesh", "blk", None, None),
        P("mesh", "blk", None),
    )
    return jax.shard_map(
        local, mesh=mesh, in_specs=placed,
        out_specs=P("mesh", "blk", None, None, None), check_vma=False,
    )
```

```python
import functools

import jax
import jax.numpy as jnp
from jax import lax
from jax.experimental import pallas as pl
from jax.experimental.pallas import tpu as pltpu
from jax.sharding import PartitionSpec as P

CX, CY, CZ = 8, 32, 128
PLANE = CX * CY
ITERS = 2
TURN_MOST = 7
CAP = 64
TILE = 1024
SIDE = 4
GROUPS = sorted(
    ((dy, dx) for dy in range(SIDE) for dx in range(SIDE)),
    key=lambda o: -sum(min(a, SIDE - a) for a in o),
)
ALONG_Z = (2, 1, 3, 0)
OPEN = 2
CHUNKS = 0x64210
GROUP = SIDE * CAP


def packed(values):
    word = sum(v << (2 * i) for i, v in enumerate(values))
    return word - (1 << 32) if word >= 1 << 31 else word

LANES = 128
PITCH = 132
MESH = pl.DeviceIdType.MESH
BF = jnp.bfloat16
F32 = jnp.float32


def iota(shape, dim):
    return lax.broadcasted_iota(jnp.int32, shape, dim)


def kernel(
    rot, n,
    fs, kap, st, db, df, fc, out,
    F0, KV, SV, SB, SF, SC, A3, WH, WL, WZ, ZO, QO, QV, E, NN, V2,
    EP, CS, IN, R, G, D, V, FR, NS, VE, GOT, MID, CARRY,
    sendS, recvS, sendH, recvH,
    in_sem, s_sem, r_sem, hs_sem, hr_sem, m_sem,
):
    m = lax.axis_index("mesh")
    d = lax.axis_index("blk")
    slots = n * CAP
    tiles = slots // TILE
    moved = m == 1

    def near(delta):
        return (d + delta) & (n - 1)

    loads = [
        pltpu.make_async_copy(src, dst, in_sem.at[i])
        for i, (src, dst) in enumerate(
            ((db, SB), (df, SF), (fc, SC.at[0]), (fs, F0), (kap, KV.at[0]), (st, SV.at[0]))
        )
    ]
    for copy in loads:
        copy.start()

    py = [(((d >> 4) + o) & 3) << 4 for o in range(SIDE)]
    px = [(((d >> 2) + o) & 3) << 2 for o in range(SIDE)]
    pz = [(d + o) & 3 for o in range(SIDE)]
    barrier = pltpu.get_barrier_semaphore()
    for dy, dx in GROUPS:
        for dz in ALONG_Z:
            pl.semaphore_signal(barrier, inc=1, device_id=(1 - m, py[dy] + px[dx] + pz[dz]), device_id_type=MESH)
    deltas = sorted({s * k for s in (1, -1) for k in (1, rot, rot + 1, rot - 1) if k})
    for delta in deltas:
        pl.semaphore_signal(barrier, inc=1, device_id=(m, near(delta)), device_id_type=MESH)

    for copy in loads[:3]:
        copy.wait()
    turn = (slots - rot * CAP) % slots

    def turned(x):
        return jnp.where(m == 0, pltpu.roll(x, turn, axis=1), x)

    SB[...] = turned(SB[...])
    SC[0] = turned(SC[0])
    for i in range(3):
        SF[:, i * slots : (i + 1) * slots] = turned(SF[:, i * slots : (i + 1) * slots])

    def hat(count, at, frac):
        i = iota((count, GROUP), 0)
        return jnp.where(i == at, 1.0 - frac, jnp.where(i == at + 1, frac, 0.0))

    def weigh(g):
        cols = pl.ds(pl.multiple_of(g * GROUP, GROUP), GROUP)
        b = SB[:, cols]
        fz, fx, fy = (SF[:, pl.ds(pl.multiple_of(i * slots + g * GROUP, GROUP), GROUP)] for i in range(3))
        hx, hy = hat(CX, (b >> 5) & 7, fx), hat(CY, b & 31, fy)
        for i in range(CX):
            w = hx[i : i + 1] * hy
            hi = w.astype(BF)
            WH[i * CY : (i + 1) * CY, cols] = hi
            WL[i * CY : (i + 1) * CY, cols] = (w - hi.astype(F32)).astype(BF)
        WZ[:, cols] = hat(CZ, b >> 8, fz)

    def split(h, x):
        hi = x.astype(BF)
        A3[:, h * LANES : (h + 1) * LANES] = hi
        A3[:, PLANE + h * LANES : PLANE + (h + 1) * LANES] = (x - hi.astype(F32)).astype(BF)
        A3[:, 2 * PLANE + h * LANES : 2 * PLANE + (h + 1) * LANES] = hi

    lane1 = iota((CZ, LANES), 1)
    y4 = lane1 & 31
    fringe = (y4 == 0) | (y4 == CY - 1)

    def pack(it, get):
        sl, sr = get(0, 0), pltpu.roll(get(1, 0), 32, axis=1)
        for f in range(1, 4):
            here = (lane1 >> 5) == f
            sl = jnp.where(here, pltpu.roll(get(0, f), 32 * f, axis=1), sl)
            sr = jnp.where(here, pltpu.roll(get(1, f), (32 * f + 32) % 128, axis=1), sr)
        sendH[it, 0] = sl
        sendH[it, 1] = sr

    def rows_of(h, f):
        return slice((h * 4 + f) * PITCH, (h * 4 + f) * PITCH + CZ)

    BLOCKS = [(h, f) for h in range(2) for f in range(4)]

    def at(z):
        return pl.ds(z, 8, stride=PITCH)

    top, low = CZ // 2 - 1, CZ // 2

    def solve(V):
        def forward(i, carry):
            a, b = carry
            for u in range(8):
                z = i * 8 + u
                a = (R[at(z)] + a) * G[at(z)]
                b = (R[at(CZ - 1 - z)] + b) * G[at(CZ - 1 - z)]
                D[at(z)] = a
                D[at(CZ - 1 - z)] = b
            return a, b

        zero = jnp.zeros((8, LANES), F32)
        a, b = lax.fori_loop(0, CZ // 16, forward, (zero, zero))
        a = (a + G[at(top)] * b) * MID[...]
        b = b + G[at(low)] * a
        V[at(top)] = a
        V[at(low)] = b

        def backward(i, carry):
            a, b = carry
            for u in range(9):
                z = i * 9 + u + 1
                a = D[at(top - z)] + G[at(top - z)] * a
                b = D[at(low + z)] + G[at(low + z)] * b
                V[at(top - z)] = a
                V[at(low + z)] = b
            return a, b

        lax.fori_loop(0, 7, backward, (a, b))

    def from_within():
        NS[...] = jnp.dot(A3[:, : 2 * PLANE], NN[...], preferred_element_type=F32)
        for h, f in BLOCKS:
            x = NS[f * CZ : (f + 1) * CZ, h * LANES : (h + 1) * LANES]
            R[rows_of(h, f)] = IN[rows_of(h, f)] + CS[rows_of(h, f)] * x

    loads[3].wait()
    pack(0, lambda h, f: F0[f * CZ : (f + 1) * CZ, h * LANES : (h + 1) * LANES])
    for h in range(2):
        split(h, F0[:, h * LANES : (h + 1) * LANES])

    early = pltpu.make_async_remote_copy(
        src_ref=VE, dst_ref=GOT, send_sem=m_sem.at[0], recv_sem=m_sem.at[1],
        device_id=(m, near(rot)), device_id_type=MESH,
    )
    carried = [
        pltpu.make_async_remote_copy(
            src_ref=src, dst_ref=dst, send_sem=m_sem.at[2 + 2 * i], recv_sem=m_sem.at[3 + 2 * i],
            device_id=(m, near(rot)), device_id_type=MESH,
        )
        for i, (src, dst) in enumerate(((SC.at[0], SC.at[1]), *((CARRY.at[k], CARRY.at[3 + k]) for k in range(3))))
    ]

    def packing(h):
        c = lane1 & 63
        inner = (((c - 32) >> 1) + (1 - h)) * CY + jnp.where(c & 1 == 0, 1, CY - 2)
        return jnp.where(c < 32, c + 96 * h, inner & 127)

    def unpacking(h):
        x, y = lane1 >> 5, lane1 & 31
        outer = x == 3 * h
        place = jnp.where(outer, y, 32 + (x - (1 - h)) * 2 + (y >> 4)) + 64 * h
        return place & 127, outer | (y == 1) | (y == CY - 2)

    def gather(x, index):
        return jnp.take_along_axis(x, index, axis=1, mode="promise_in_bounds")

    planes = [(KV, 0, 1.0), (KV, CZ, 1.0), (SV, 0, 1000.0)]

    @pl.when(moved)
    def _():
        for copy in loads[4:]:
            copy.wait()
        for k, (ref, r, _) in enumerate(planes):
            a, b = (gather(ref[0, r : r + CZ, h * LANES : (h + 1) * LANES], packing(h)) for h in range(2))
            CARRY[k] = jnp.where(lane1 < 64, a, b)

    @pl.loop(0, ITERS)
    def _(it):
        ahead = (it > 0) & moved
        edge = [(sendH.at[it, e], recvH.at[it, e]) for e in range(2)]

        def halo(e, delta):
            return pltpu.make_async_remote_copy(
                src_ref=edge[e][0], dst_ref=edge[e][1],
                send_sem=hs_sem.at[it, e], recv_sem=hr_sem.at[it, e],
                device_id=(m, near(delta)), device_id_type=MESH,
            )

        @pl.when(ahead)
        def _():
            from_within()
            for k in range(8):
                VE[k * PITCH + CZ : (k + 1) * PITCH] = jnp.zeros((PITCH - CZ, LANES), F32)
            solve(VE)
            R[...] = jnp.zeros_like(R)

        def part(u):
            rows = pl.ds(u * PITCH, PITCH)
            return pltpu.make_async_remote_copy(
                src_ref=VE.at[rows], dst_ref=GOT.at[rows], send_sem=m_sem.at[0], recv_sem=m_sem.at[1],
                device_id=(m, near(rot)), device_id_type=MESH,
            )

        def chunk_at(t):
            return (CHUNKS >> (4 * t)) & 15

        def group(k):
            dy, dx = (packed([g[0] for g in GROUPS]) >> (2 * k)) & 3, (packed([g[1] for g in GROUPS]) >> (2 * k)) & 3
            return ((((d >> 4) + dy) & 3) << 2) + (((d >> 2) + dx) & 3)

        per = TILE // GROUP
        shift = jnp.where((it > 0) & (m == 0), rot, 0)

        def send(t):
            for j in range(per):
                g = group(t * per + j)
                for dz in ALONG_Z:
                    pltpu.make_async_remote_copy(
                        src_ref=sendS.at[it, pz[dz] & 1, g * 2 + (pz[dz] >> 1)], dst_ref=recvS.at[it, d],
                        send_sem=s_sem.at[it], recv_sem=r_sem.at[it],
                        device_id=(1 - m, (g * SIDE + pz[dz] + shift) & (n - 1)), device_id_type=MESH,
                    ).start()

        @pl.loop(0, tiles)
        def _(t):
            @pl.when((it == 0) & (t == OPEN))
            def _():
                pl.semaphore_wait(barrier, n + len(deltas))

                @pl.loop(0, OPEN - 1)
                def _(u):
                    send(u)

            begin = t == jnp.where(it == 0, OPEN, 0)

            @pl.when(begin & jnp.logical_not(ahead))
            def _():
                halo(0, -1).start()
                halo(1, 1).start()

            @pl.when(begin & ahead)
            def _():
                if rot == 1:
                    pltpu.make_async_copy(edge[0][0], edge[0][1], hr_sem.at[it, 0]).start()
                else:
                    halo(0, rot - 1).start()
                halo(1, rot + 1).start()

            @pl.when(((it > 0) & (t > 0)) | (t >= OPEN))
            def _():
                send(t - 1)

            @pl.when((it == 0) & (t == OPEN) & moved)
            def _():
                carried[0].start()
                carried[1].start()

            @pl.when((it == 0) & (t == OPEN + 1) & moved)
            def _():
                carried[2].start()

            @pl.when(ahead)
            def _():
                @pl.loop(chunk_at(t), chunk_at(t + 1))
                def _(u):
                    part(u).start()

            @pl.when(it == 0)
            def _():
                @pl.loop(0, per)
                def _(j):
                    weigh(group(t * per + j))

            cols = [pl.ds(pl.multiple_of(group(t * per + j) * GROUP, GROUP), GROUP) for j in range(per)]

            def gathered(ref):
                return jnp.concatenate([ref[:, c] for c in cols], axis=1)

            wh = gathered(WH)
            p = jnp.dot(A3[...], jnp.concatenate([wh, wh, gathered(WL)], axis=0), preferred_element_type=F32)
            s = jnp.sum(p.reshape(4, CZ, TILE) * gathered(WZ)[None], axis=1)
            first = iota((2, LANES), 1) < CAP
            for j in range(per):
                g = group(t * per + j)
                for i in range(2):
                    x = s[:, j * GROUP + i * LANES : j * GROUP + (i + 1) * LANES]
                    y = pltpu.roll(x, CAP, axis=1)
                    sendS[it, 0, g * 2 + i] = jnp.where(first, x[:2], y[2:])
                    sendS[it, 1, g * 2 + i] = jnp.where(first, y[:2], x[2:])

        send(tiles - 1)

        @pl.when(ahead)
        def _():
            @pl.loop(chunk_at(tiles), 8)
            def _(u):
                part(u).start()

        @pl.when((it == 0) & moved)
        def _():
            carried[3].start()

        @pl.when((it == 0) & (m == 0))
        def _():
            for copy in loads[4:]:
                copy.wait()
            GOT[...] = jnp.zeros_like(GOT)

        @pl.when(it == 0)
        def _():
            row, col = iota((128, 2 * 2 * 4 * LANES), 0), iota((128, 2 * 2 * 4 * LANES), 1)
            q = row & 15
            kind, half, fld, lane = col >> 10, (col >> 9) & 1, (col >> 7) & 3, col & 127
            place = (q >> 1) * CY + (q & 1) * (CY - 1) + kind * (1 - 2 * (q & 1))
            E[...] = jnp.where((((row >> 4) & 3) == fld) & (half * LANES + lane == place), 1.0, 0.0).astype(BF)
            src, dst = iota((512, 256), 0) & 255, iota((512, 256), 1)
            gap = jnp.abs(src - dst)
            sy, dy = src & 31, dst & 31
            rim = (sy == 0) | (sy == CY - 1) | (dy == 0) | (dy == CY - 1)
            NN[...] = jnp.where(((gap == 1) | (gap == CY)) & ~rim, 1.0, 0.0).astype(BF)

        @pl.when(ahead)
        def _():
            for copy in carried:
                copy.wait()
            for k, (ref, r, other) in enumerate(planes):
                for h in range(2):
                    index, used = unpacking(h)
                    ref[1, r : r + CZ, h * LANES : (h + 1) * LANES] = jnp.where(used, gather(CARRY[3 + k], index), other)

        @pl.when((it == 0) | moved)
        def _():
            @pl.loop(0, n // SIDE)
            def _(g):
                cols = pl.ds(pl.multiple_of(g * GROUP, GROUP), GROUP)
                c = SC[it, :, cols]
                ZO[:, cols] = jnp.where(iota((CZ, GROUP), 0) == (c >> 8), 1.0, 0.0).astype(BF)
                cq = ((c >> 5) & 7) * 2 + jnp.where((c & 31) == 0, 0, 1)
                QO[:, cols] = jnp.where(iota((16, GROUP), 0) == cq, 1.0, 0.0)

            for h in range(2):
                lanes = slice(h * LANES, (h + 1) * LANES)
                inv = 1.0 / SV[it, :, lanes]
                for f in range(4):
                    k = f // 3
                    c = KV[it, k * CZ : (k + 1) * CZ, lanes]
                    EP[rows_of(h, f)] = (1.0 + 4.0 * c) * inv
                    CS[rows_of(h, f)] = c * inv
                    IN[rows_of(h, f)] = F0[f * CZ : (f + 1) * CZ, lanes] * inv

            def factor(i, carry):
                ha, hb = carry
                for u in range(8):
                    z = i * 8 + u
                    ta, tb = EP[at(z)] + ha, EP[at(CZ - 1 - z)] + hb
                    ga, gb = 1.0 / (1.0 + ta), 1.0 / (1.0 + tb)
                    G[at(z)] = ga
                    G[at(CZ - 1 - z)] = gb
                    ha, hb = ta * ga, tb * gb
                return ha, hb

            one = jnp.ones((8, LANES), F32)
            ha, hb = lax.fori_loop(0, CZ // 16, factor, (one, one))
            MID[...] = 1.0 / (ha + hb - ha * hb)

        @pl.when(jnp.logical_not(ahead))
        def _():
            from_within()

        for e in range(2):
            halo(e, 1).wait_recv()
        halo(1, 1).wait_send()
        if rot == 1:

            @pl.when(jnp.logical_not(ahead))
            def _():
                halo(0, 1).wait_send()
        else:
            halo(0, 1).wait_send()
        hr, hl = recvH[it, 0], recvH[it, 1]
        for h, f in BLOCKS:
            if h == 0:
                x = jnp.where(lane1 < 32, pltpu.roll(hl, (128 - 32 * f) % 128, axis=1), 0.0)
            else:
                x = jnp.where(lane1 >= 96, pltpu.roll(hr, 96 - 32 * f, axis=1), 0.0)
            R[rows_of(h, f)] = R[rows_of(h, f)] + CS[rows_of(h, f)] * x

        pltpu.make_async_copy(recvS.at[it], recvS.at[it], r_sem.at[it]).wait()
        got = recvS[it].reshape(n // 4, 8, LANES)
        front = (iota(got.shape, 1) & 2) == 0
        turned = pltpu.roll(got, CAP, axis=2)
        turned = jnp.where(front, pltpu.roll(turned, 6, axis=1), pltpu.roll(turned, 2, axis=1))
        rest = jnp.where((iota(got.shape, 2) < CAP) == front, got, turned).reshape(2 * n, LANES)
        for piece in range(2):
            part = rest.astype(BF).astype(F32)
            rest = rest - part
            V2[piece] = part
        for i in range(n // 2):
            cols = slice(i * LANES, (i + 1) * LANES)
            for piece in range(2):
                for f in range(4):
                    r = piece * 64 + f * 16
                    QV[r : r + 16, cols] = (QO[:, cols] * V2[piece, i * 4 + f : i * 4 + f + 1]).astype(BF)
        dp = lax.dot_general(ZO[...], QV[...], (((1,), (1,)), ((), ())), preferred_element_type=F32).astype(BF)
        for h in range(2):
            fr = jnp.dot(dp, E[:, h * 512 : (h + 1) * 512], preferred_element_type=F32)
            nb = jnp.dot(dp, E[:, 1024 + h * 512 : 1024 + (h + 1) * 512], preferred_element_type=F32)
            for f in range(4):
                FR[rows_of(h, f)] = fr[:, f * LANES : (f + 1) * LANES]
                R[rows_of(h, f)] = R[rows_of(h, f)] + CS[rows_of(h, f)] * nb[:, f * LANES : (f + 1) * LANES]
        solve(V)

        pltpu.make_async_copy(recvS.at[it], recvS.at[it], s_sem.at[it]).wait()

        @pl.when(it < ITERS - 1)
        def _():
            def new(h, f):
                return jnp.where(fringe, FR[rows_of(h, f)], V[rows_of(h, f)])

            pack(it + 1, new)
            for h in range(2):
                split(h, jnp.concatenate([new(h, f) for f in range(4)], axis=0))

    @pl.when(moved)
    def _():
        early.wait()

    for h, f in BLOCKS:
        out[f * CZ : (f + 1) * CZ, h * LANES : (h + 1) * LANES] = jnp.where(
            fringe, FR[rows_of(h, f)], V[rows_of(h, f)] + GOT[rows_of(h, f)]
        )


def step(rot, n, args):
    slots = n * CAP
    vm = pltpu.VMEM
    dma = pltpu.SemaphoreType.DMA
    tall = vm((8 * PITCH, LANES), F32)
    return pl.pallas_call(
        functools.partial(kernel, rot, n),
        out_shape=jax.ShapeDtypeStruct((4 * CZ, PLANE), F32),
        in_specs=[pl.BlockSpec(memory_space=pl.ANY)] * 6,
        out_specs=pl.BlockSpec(memory_space=pltpu.VMEM),
        scratch_shapes=[
            vm((512, 256), F32), vm((2, 256, 256), F32), vm((2, 128, 256), F32),
            vm((1, slots), jnp.int32), vm((1, 3 * slots), F32), vm((2, 1, slots), jnp.int32),
            vm((512, 768), BF), vm((256, slots), BF), vm((256, slots), BF), vm((CZ, slots), F32), vm((CZ, slots), BF),
            vm((16, slots), F32), vm((128, slots), BF), vm((128, 2048), BF), vm((512, 256), BF),
            vm((2, 2 * n, LANES), F32),
            tall, tall, tall, tall, tall, tall, tall, tall,
            vm((512, 256), F32), tall, tall, vm((8, LANES), F32), vm((6, CZ, LANES), F32),
            vm((ITERS, 2, n // 2, 2, LANES), F32), vm((ITERS, n, 2, LANES), F32),
            vm((ITERS, 2, CZ, LANES), F32), vm((ITERS, 2, CZ, LANES), F32),
            dma((6,)), dma((ITERS,)), dma((ITERS,)), dma((ITERS, 2)), dma((ITERS, 2)), dma((10,)),
        ],
        compiler_params=pltpu.CompilerParams(collective_id=rot, has_side_effects=True),
        name=f"rotor_step_{rot}",
    )(*args)


def solution(mesh):
    n = mesh.shape["blk"]

    def local(rotation_step, field_state, diffusivity, stretch, donor_base, donor_frac, fringe_cell):
        slots = n * CAP
        args = (
            field_state.reshape(4 * CZ, PLANE),
            diffusivity.reshape(2 * CZ, PLANE),
            stretch.reshape(CZ, PLANE),
            donor_base.reshape(1, slots),
            donor_frac.reshape(1, 3 * slots),
            fringe_cell.reshape(1, slots),
        )
        branches = [functools.partial(lambda rot, a: step(rot, n, a), rot) for rot in range(1, TURN_MOST + 1)]
        new = lax.switch(jnp.clip(rotation_step[0] - 1, 0, TURN_MOST - 1), branches, args)
        return new.reshape(1, 1, 4, CZ, PLANE)

    placed = (
        P(),
        P("mesh", "blk", None, None, None),
        P("mesh", "blk", None, None, None),
        P("mesh", "blk", None, None),
        P("mesh", "blk", None),
        P("mesh", "blk", None, None),
        P("mesh", "blk", None),
    )
    return jax.shard_map(
        local, mesh=mesh, in_specs=placed,
        out_specs=P("mesh", "blk", None, None, None), check_vma=False,
    )
```

```python
import functools

import jax
import jax.numpy as jnp
from jax import lax
from jax.experimental import pallas as pl
from jax.experimental.pallas import tpu as pltpu
from jax.sharding import PartitionSpec as P

CX, CY, CZ = 8, 32, 128
PLANE = CX * CY
ITERS = 2
TURN_MOST = 7
CAP = 64
TILE = 1024
SIDE = 4
GROUPS = sorted(
    ((dy, dx) for dy in range(SIDE) for dx in range(SIDE)),
    key=lambda o: -sum(min(a, SIDE - a) for a in o),
)
ALONG_Z = (2, 1, 3, 0)
OPEN = 2
CHUNKS = 0x64210
GROUP = SIDE * CAP


def packed(values):
    word = sum(v << (2 * i) for i, v in enumerate(values))
    return word - (1 << 32) if word >= 1 << 31 else word

LANES = 128
PITCH = 132
MESH = pl.DeviceIdType.MESH
BF = jnp.bfloat16
F32 = jnp.float32


def iota(shape, dim):
    return lax.broadcasted_iota(jnp.int32, shape, dim)


def kernel(
    rot, n,
    fs, kap, st, db, df, fc, out,
    F0, KV, SV, SB, SF, SC, A3, WH, WL, WZ, ZO, QO, QV, NN, V2,
    EP, CS, IN, R, G, D, V, FR, NS, VE, GOT, MID, CARRY,
    sendS, recvS, sendH, recvH,
    in_sem, s_sem, r_sem, hs_sem, hr_sem, m_sem,
):
    m = lax.axis_index("mesh")
    d = lax.axis_index("blk")
    slots = n * CAP
    tiles = slots // TILE
    moved = m == 1

    def near(delta):
        return (d + delta) & (n - 1)

    loads = [
        pltpu.make_async_copy(src, dst, in_sem.at[i])
        for i, (src, dst) in enumerate(
            ((db, SB), (df, SF), (fc, SC.at[0]), (fs, F0), (kap, KV.at[0]), (st, SV.at[0]))
        )
    ]
    for copy in loads:
        copy.start()

    py = [(((d >> 4) + o) & 3) << 4 for o in range(SIDE)]
    px = [(((d >> 2) + o) & 3) << 2 for o in range(SIDE)]
    pz = [(d + o) & 3 for o in range(SIDE)]
    barrier = pltpu.get_barrier_semaphore()
    for dy, dx in GROUPS:
        for dz in ALONG_Z:
            pl.semaphore_signal(barrier, inc=1, device_id=(1 - m, py[dy] + px[dx] + pz[dz]), device_id_type=MESH)
    deltas = sorted({s * k for s in (1, -1) for k in (1, rot, rot + 1, rot - 1) if k})
    for delta in deltas:
        pl.semaphore_signal(barrier, inc=1, device_id=(m, near(delta)), device_id_type=MESH)

    for copy in loads[:3]:
        copy.wait()
    turn = (slots - rot * CAP) % slots

    def turned(x):
        return jnp.where(m == 0, pltpu.roll(x, turn, axis=1), x)

    SB[...] = turned(SB[...])
    SC[0] = turned(SC[0])
    for i in range(3):
        SF[:, i * slots : (i + 1) * slots] = turned(SF[:, i * slots : (i + 1) * slots])

    def hat(count, at, frac):
        i = iota((count, GROUP), 0)
        return jnp.where(i == at, 1.0 - frac, jnp.where(i == at + 1, frac, 0.0))

    def weigh(g):
        cols = pl.ds(pl.multiple_of(g * GROUP, GROUP), GROUP)
        b = SB[:, cols]
        fz, fx, fy = (SF[:, pl.ds(pl.multiple_of(i * slots + g * GROUP, GROUP), GROUP)] for i in range(3))
        hx, hy = hat(CX, (b >> 5) & 7, fx), hat(CY, b & 31, fy)
        for i in range(CX):
            w = hx[i : i + 1] * hy
            hi = w.astype(BF)
            WH[i * CY : (i + 1) * CY, cols] = hi
            WL[i * CY : (i + 1) * CY, cols] = (w - hi.astype(F32)).astype(BF)
        WZ[:, cols] = hat(CZ, b >> 8, fz)

    def split(h, x):
        hi = x.astype(BF)
        A3[:, h * LANES : (h + 1) * LANES] = hi
        A3[:, PLANE + h * LANES : PLANE + (h + 1) * LANES] = (x - hi.astype(F32)).astype(BF)

    lane1 = iota((CZ, LANES), 1)
    y4 = lane1 & 31
    fringe = (y4 == 0) | (y4 == CY - 1)

    def pack(it, get):
        sl, sr = get(0, 0), pltpu.roll(get(1, 0), 32, axis=1)
        for f in range(1, 4):
            here = (lane1 >> 5) == f
            sl = jnp.where(here, pltpu.roll(get(0, f), 32 * f, axis=1), sl)
            sr = jnp.where(here, pltpu.roll(get(1, f), (32 * f + 32) % 128, axis=1), sr)
        sendH[it, 0] = sl
        sendH[it, 1] = sr

    def rows_of(h, f):
        return slice((h * 4 + f) * PITCH, (h * 4 + f) * PITCH + CZ)

    BLOCKS = [(h, f) for h in range(2) for f in range(4)]

    def new(h, f):
        return jnp.where(fringe, FR[rows_of(h, f)], V[rows_of(h, f)])

    def at(z):
        return pl.ds(z, 8, stride=PITCH)

    top, low = CZ // 2 - 1, CZ // 2

    def solve(V):
        def forward(i, carry):
            a, b = carry
            for u in range(8):
                z = i * 8 + u
                a = (R[at(z)] + a) * G[at(z)]
                b = (R[at(CZ - 1 - z)] + b) * G[at(CZ - 1 - z)]
                D[at(z)] = a
                D[at(CZ - 1 - z)] = b
            return a, b

        zero = jnp.zeros((8, LANES), F32)
        a, b = lax.fori_loop(0, CZ // 16, forward, (zero, zero))
        a = (a + G[at(top)] * b) * MID[...]
        b = b + G[at(low)] * a
        V[at(top)] = a
        V[at(low)] = b

        def backward(i, carry):
            a, b = carry
            for u in range(9):
                z = i * 9 + u + 1
                a = D[at(top - z)] + G[at(top - z)] * a
                b = D[at(low + z)] + G[at(low + z)] * b
                V[at(top - z)] = a
                V[at(low + z)] = b
            return a, b

        lax.fori_loop(0, 7, backward, (a, b))

    def from_within():
        NS[...] = jnp.dot(A3[...], NN[...], preferred_element_type=F32)
        for h, f in BLOCKS:
            x = NS[f * CZ : (f + 1) * CZ, h * LANES : (h + 1) * LANES]
            R[rows_of(h, f)] = IN[rows_of(h, f)] + CS[rows_of(h, f)] * x

    loads[3].wait()
    pack(0, lambda h, f: F0[f * CZ : (f + 1) * CZ, h * LANES : (h + 1) * LANES])
    for h in range(2):
        split(h, F0[:, h * LANES : (h + 1) * LANES])

    early = pltpu.make_async_remote_copy(
        src_ref=VE, dst_ref=GOT, send_sem=m_sem.at[0], recv_sem=m_sem.at[1],
        device_id=(m, near(rot)), device_id_type=MESH,
    )
    carried = [
        pltpu.make_async_remote_copy(
            src_ref=src, dst_ref=dst, send_sem=m_sem.at[2 + 2 * i], recv_sem=m_sem.at[3 + 2 * i],
            device_id=(m, near(rot)), device_id_type=MESH,
        )
        for i, (src, dst) in enumerate(((SC.at[0], SC.at[1]), *((CARRY.at[k], CARRY.at[3 + k]) for k in range(3))))
    ]

    def packing(h):
        c = lane1 & 63
        inner = (((c - 32) >> 1) + (1 - h)) * CY + jnp.where(c & 1 == 0, 1, CY - 2)
        return jnp.where(c < 32, c + 96 * h, inner & 127)

    def unpacking(h):
        x, y = lane1 >> 5, lane1 & 31
        outer = x == 3 * h
        place = jnp.where(outer, y, 32 + (x - (1 - h)) * 2 + (y >> 4)) + 64 * h
        return place & 127, outer | (y == 1) | (y == CY - 2)

    def gather(x, index):
        return jnp.take_along_axis(x, index, axis=1, mode="promise_in_bounds")

    planes = [(KV, 0, 1.0), (KV, CZ, 1.0), (SV, 0, 1000.0)]

    @pl.when(moved)
    def _():
        for copy in loads[4:]:
            copy.wait()
        for k, (ref, r, _) in enumerate(planes):
            a, b = (gather(ref[0, r : r + CZ, h * LANES : (h + 1) * LANES], packing(h)) for h in range(2))
            CARRY[k] = jnp.where(lane1 < 64, a, b)

    @pl.loop(0, ITERS)
    def _(it):
        ahead = (it > 0) & moved
        edge = [(sendH.at[it, e], recvH.at[it, e]) for e in range(2)]

        def halo(e, delta):
            return pltpu.make_async_remote_copy(
                src_ref=edge[e][0], dst_ref=edge[e][1],
                send_sem=hs_sem.at[it, e], recv_sem=hr_sem.at[it, e],
                device_id=(m, near(delta)), device_id_type=MESH,
            )

        def part(u):
            rows = pl.ds(u * PITCH, PITCH)
            return pltpu.make_async_remote_copy(
                src_ref=VE.at[rows], dst_ref=GOT.at[rows], send_sem=m_sem.at[0], recv_sem=m_sem.at[1],
                device_id=(m, near(rot)), device_id_type=MESH,
            )

        def chunk_at(t):
            return (CHUNKS >> (4 * t)) & 15

        def group(k):
            dy, dx = (packed([g[0] for g in GROUPS]) >> (2 * k)) & 3, (packed([g[1] for g in GROUPS]) >> (2 * k)) & 3
            return ((((d >> 4) + dy) & 3) << 2) + (((d >> 2) + dx) & 3)

        per = TILE // GROUP
        shift = jnp.where((it > 0) & (m == 0), rot, 0)

        def send(t):
            for j in range(per):
                g = group(t * per + j)
                for dz in ALONG_Z:
                    pltpu.make_async_remote_copy(
                        src_ref=sendS.at[it, pz[dz] & 1, g * 2 + (pz[dz] >> 1)], dst_ref=recvS.at[it, d],
                        send_sem=s_sem.at[it], recv_sem=r_sem.at[it],
                        device_id=(1 - m, (g * SIDE + pz[dz] + shift) & (n - 1)), device_id_type=MESH,
                    ).start()

        @pl.loop(0, tiles)
        def _(t):
            @pl.when((it == 0) & (t == OPEN))
            def _():
                pl.semaphore_wait(barrier, n + len(deltas))

                @pl.loop(0, OPEN - 1)
                def _(u):
                    send(u)

            @pl.when((it == 0) & (t == OPEN))
            def _():
                halo(0, -1).start()
                halo(1, 1).start()

            @pl.when(((it > 0) & (t > 0)) | (t >= OPEN))
            def _():
                send(t - 1)

            @pl.when((it > 0) & (t == 0))
            def _():
                pack(it, new)

            @pl.when((it > 0) & (t == 0) & (m == 0))
            def _():
                halo(0, -1).start()
                halo(1, 1).start()

            @pl.when(ahead & (t == 0))
            def _():
                if rot == 1:
                    pltpu.make_async_copy(edge[0][0], edge[0][1], hr_sem.at[it, 0]).start()
                else:
                    halo(0, rot - 1).start()
                halo(1, rot + 1).start()
                from_within()
                for k in range(8):
                    VE[k * PITCH + CZ : (k + 1) * PITCH] = jnp.zeros((PITCH - CZ, LANES), F32)
                solve(VE)
                R[...] = jnp.zeros_like(R)

            @pl.when((it == 0) & (t == OPEN) & moved)
            def _():
                carried[0].start()
                carried[1].start()

            @pl.when((it == 0) & (t == OPEN + 1) & moved)
            def _():
                carried[2].start()

            @pl.when(ahead)
            def _():
                @pl.loop(chunk_at(t), chunk_at(t + 1))
                def _(u):
                    part(u).start()

            @pl.when((it == 0) & (t == 0))
            def _():
                pl.loop(0, n // SIDE)(weigh)

            cols = [pl.ds(pl.multiple_of(group(t * per + j) * GROUP, GROUP), GROUP) for j in range(per)]

            def gathered(ref):
                return jnp.concatenate([ref[:, c] for c in cols], axis=1)

            wh = gathered(WH)
            a3 = jnp.concatenate([A3[...], A3[:, :PLANE]], axis=1)
            p = jnp.dot(a3, jnp.concatenate([wh, wh, gathered(WL)], axis=0), preferred_element_type=F32)
            s = jnp.sum(p.reshape(4, CZ, TILE) * gathered(WZ)[None], axis=1)
            first = iota((2, LANES), 1) < CAP
            for j in range(per):
                g = group(t * per + j)
                for i in range(2):
                    x = s[:, j * GROUP + i * LANES : j * GROUP + (i + 1) * LANES]
                    y = pltpu.roll(x, CAP, axis=1)
                    sendS[it, 0, g * 2 + i] = jnp.where(first, x[:2], y[2:])
                    sendS[it, 1, g * 2 + i] = jnp.where(first, y[:2], x[2:])

        send(tiles - 1)

        @pl.when(ahead)
        def _():
            @pl.loop(chunk_at(tiles), 8)
            def _(u):
                part(u).start()

        @pl.when((it == 0) & moved)
        def _():
            carried[3].start()

        @pl.when((it == 0) & (m == 0))
        def _():
            for copy in loads[4:]:
                copy.wait()
            GOT[...] = jnp.zeros_like(GOT)

        @pl.when(it == 0)
        def _():
            src, dst = iota((512, 256), 0) & 255, iota((512, 256), 1)
            gap = jnp.abs(src - dst)
            sy, dy = src & 31, dst & 31
            rim = (sy == 0) | (sy == CY - 1) | (dy == 0) | (dy == CY - 1)
            NN[...] = jnp.where(((gap == 1) | (gap == CY)) & ~rim, 1.0, 0.0).astype(BF)

        @pl.when(ahead)
        def _():
            for copy in carried:
                copy.wait()
            for k, (ref, r, other) in enumerate(planes):
                for h in range(2):
                    index, used = unpacking(h)
                    ref[1, r : r + CZ, h * LANES : (h + 1) * LANES] = jnp.where(used, gather(CARRY[3 + k], index), other)

        @pl.when((it == 0) | moved)
        def _():
            @pl.loop(0, n // SIDE)
            def _(g):
                cols = pl.ds(pl.multiple_of(g * GROUP, GROUP), GROUP)
                c = SC[it, :, cols]
                ZO[:, cols] = jnp.where(iota((CZ, GROUP), 0) == (c >> 8), 1.0, 0.0).astype(BF)
                cq = ((c >> 5) & 7) * 2 + jnp.where((c & 31) == 0, 0, 1)
                QO[:, cols] = jnp.where(iota((16, GROUP), 0) == cq, 1.0, 0.0)

            for h in range(2):
                lanes = slice(h * LANES, (h + 1) * LANES)
                inv = 1.0 / SV[it, :, lanes]
                for f in range(4):
                    k = f // 3
                    c = KV[it, k * CZ : (k + 1) * CZ, lanes]
                    EP[rows_of(h, f)] = (1.0 + 4.0 * c) * inv
                    CS[rows_of(h, f)] = c * inv
                    IN[rows_of(h, f)] = F0[f * CZ : (f + 1) * CZ, lanes] * inv

            def factor(i, carry):
                ha, hb = carry
                for u in range(8):
                    z = i * 8 + u
                    ta, tb = EP[at(z)] + ha, EP[at(CZ - 1 - z)] + hb
                    ga, gb = 1.0 / (1.0 + ta), 1.0 / (1.0 + tb)
                    G[at(z)] = ga
                    G[at(CZ - 1 - z)] = gb
                    ha, hb = ta * ga, tb * gb
                return ha, hb

            one = jnp.ones((8, LANES), F32)
            ha, hb = lax.fori_loop(0, CZ // 16, factor, (one, one))
            MID[...] = 1.0 / (ha + hb - ha * hb)

        @pl.when(jnp.logical_not(ahead))
        def _():
            from_within()

        for e in range(2):
            halo(e, 1).wait_recv()
        halo(1, 1).wait_send()
        if rot == 1:

            @pl.when(jnp.logical_not(ahead))
            def _():
                halo(0, 1).wait_send()
        else:
            halo(0, 1).wait_send()
        hr, hl = recvH[it, 0], recvH[it, 1]
        for h, f in BLOCKS:
            if h == 0:
                x = jnp.where(lane1 < 32, pltpu.roll(hl, (128 - 32 * f) % 128, axis=1), 0.0)
            else:
                x = jnp.where(lane1 >= 96, pltpu.roll(hr, 96 - 32 * f, axis=1), 0.0)
            R[rows_of(h, f)] = R[rows_of(h, f)] + CS[rows_of(h, f)] * x

        pltpu.make_async_copy(recvS.at[it], recvS.at[it], r_sem.at[it]).wait()
        got = recvS[it].reshape(n // 4, 8, LANES)
        front = (iota(got.shape, 1) & 2) == 0
        turned = pltpu.roll(got, CAP, axis=2)
        turned = jnp.where(front, pltpu.roll(turned, 6, axis=1), pltpu.roll(turned, 2, axis=1))
        rest = jnp.where((iota(got.shape, 2) < CAP) == front, got, turned).reshape(2 * n, LANES)
        for piece in range(2):
            part = rest.astype(BF).astype(F32)
            rest = rest - part
            V2[piece] = part
        for i in range(n // 2):
            cols = slice(i * LANES, (i + 1) * LANES)
            for piece in range(2):
                for f in range(4):
                    r = piece * 64 + f * 16
                    QV[r : r + 16, cols] = (QO[:, cols] * V2[piece, i * 4 + f : i * 4 + f + 1]).astype(BF)
        dp = lax.dot_general(ZO[...], QV[...], (((1,), (1,)), ((), ())), preferred_element_type=F32)
        dp = dp + pltpu.roll(dp, CAP, axis=1)
        column = (lane1 >> 5) * 2 + (y4 >> 4)
        beside = (y4 == 1) | (y4 == CY - 2)
        for h, f in BLOCKS:
            x = gather(dp, column + (f * 16 + h * 8))
            FR[rows_of(h, f)] = x
            R[rows_of(h, f)] = R[rows_of(h, f)] + jnp.where(beside, CS[rows_of(h, f)] * x, 0.0)
        solve(V)

        pltpu.make_async_copy(recvS.at[it], recvS.at[it], s_sem.at[it]).wait()

        @pl.when(it < ITERS - 1)
        def _():
            for h in range(2):
                split(h, jnp.concatenate([new(h, f) for f in range(4)], axis=0))

    @pl.when(moved)
    def _():
        early.wait()

    for h, f in BLOCKS:
        out[f * CZ : (f + 1) * CZ, h * LANES : (h + 1) * LANES] = jnp.where(
            fringe, FR[rows_of(h, f)], V[rows_of(h, f)] + GOT[rows_of(h, f)]
        )


def step(rot, n, args):
    slots = n * CAP
    vm = pltpu.VMEM
    dma = pltpu.SemaphoreType.DMA
    tall = vm((8 * PITCH, LANES), F32)
    return pl.pallas_call(
        functools.partial(kernel, rot, n),
        out_shape=jax.ShapeDtypeStruct((4 * CZ, PLANE), F32),
        in_specs=[pl.BlockSpec(memory_space=pl.ANY)] * 6,
        out_specs=pl.BlockSpec(memory_space=pltpu.VMEM),
        scratch_shapes=[
            vm((512, 256), F32), vm((2, 256, 256), F32), vm((2, 128, 256), F32),
            vm((1, slots), jnp.int32), vm((1, 3 * slots), F32), vm((2, 1, slots), jnp.int32),
            vm((512, 512), BF), vm((256, slots), BF), vm((256, slots), BF), vm((CZ, slots), F32), vm((CZ, slots), BF),
            vm((16, slots), F32), vm((128, slots), BF), vm((512, 256), BF),
            vm((2, 2 * n, LANES), F32),
            tall, tall, tall, tall, tall, tall, tall, tall,
            vm((512, 256), F32), tall, tall, vm((8, LANES), F32), vm((6, CZ, LANES), F32),
            vm((ITERS, 2, n // 2, 2, LANES), F32), vm((ITERS, n, 2, LANES), F32),
            vm((ITERS, 2, CZ, LANES), F32), vm((ITERS, 2, CZ, LANES), F32),
            dma((6,)), dma((ITERS,)), dma((ITERS,)), dma((ITERS, 2)), dma((ITERS, 2)), dma((10,)),
        ],
        compiler_params=pltpu.CompilerParams(collective_id=rot, has_side_effects=True),
        name=f"rotor_step_{rot}",
    )(*args)


def solution(mesh):
    n = mesh.shape["blk"]

    def local(rotation_step, field_state, diffusivity, stretch, donor_base, donor_frac, fringe_cell):
        slots = n * CAP
        args = (
            field_state.reshape(4 * CZ, PLANE),
            diffusivity.reshape(2 * CZ, PLANE),
            stretch.reshape(CZ, PLANE),
            donor_base.reshape(1, slots),
            donor_frac.reshape(1, 3 * slots),
            fringe_cell.reshape(1, slots),
        )
        branches = [functools.partial(lambda rot, a: step(rot, n, a), rot) for rot in range(1, TURN_MOST + 1)]
        new = lax.switch(jnp.clip(rotation_step[0] - 1, 0, TURN_MOST - 1), branches, args)
        return new.reshape(1, 1, 4, CZ, PLANE)

    placed = (
        P(),
        P("mesh", "blk", None, None, None),
        P("mesh", "blk", None, None, None),
        P("mesh", "blk", None, None),
        P("mesh", "blk", None),
        P("mesh", "blk", None, None),
        P("mesh", "blk", None),
    )
    return jax.shard_map(
        local, mesh=mesh, in_specs=placed,
        out_specs=P("mesh", "blk", None, None, None), check_vma=False,
    )
```

```python
import functools

import jax
import jax.numpy as jnp
from jax import lax
from jax.experimental import pallas as pl
from jax.experimental.pallas import tpu as pltpu
from jax.sharding import PartitionSpec as P

CX, CY, CZ = 8, 32, 128
PLANE = CX * CY
ITERS = 2
TURN_MOST = 7
CAP = 64
TILE = 1024
SIDE = 4
GROUPS = sorted(
    ((dy, dx) for dy in range(SIDE) for dx in range(SIDE)),
    key=lambda o: -sum(min(a, SIDE - a) for a in o),
)
ALONG_Z = (2, 1, 3, 0)
NEAR, FAR = 2, 4
CHUNKS = 0x64210
GROUP = SIDE * CAP


def packed(values):
    word = sum(v << (2 * i) for i, v in enumerate(values))
    return word - (1 << 32) if word >= 1 << 31 else word

LANES = 128
PITCH = 132
MESH = pl.DeviceIdType.MESH
BF = jnp.bfloat16
F32 = jnp.float32


def iota(shape, dim):
    return lax.broadcasted_iota(jnp.int32, shape, dim)


def kernel(
    rot, n,
    fs, kap, st, db, df, fc, out,
    F0, KV, SV, SB, SF, SC, A3, WH, WL, WZ, ZO, QO, QV, NN, V2,
    EP, CS, IN, R, G, D, V, FR, NS, VE, GOT, MID, CARRY,
    sendS, recvS, sendH, recvH,
    in_sem, s_sem, r_sem, hs_sem, hr_sem, m_sem,
):
    m = lax.axis_index("mesh")
    d = lax.axis_index("blk")
    slots = n * CAP
    tiles = slots // TILE
    moved = m == 1

    def near(delta):
        return (d + delta) & (n - 1)

    loads = [
        pltpu.make_async_copy(src, dst, in_sem.at[i])
        for i, (src, dst) in enumerate(
            ((db, SB), (df, SF), (fc, SC.at[0]), (fs, F0), (kap, KV.at[0]), (st, SV.at[0]))
        )
    ]
    for copy in loads:
        copy.start()

    py = [(((d >> 4) + o) & 3) << 4 for o in range(SIDE)]
    px = [(((d >> 2) + o) & 3) << 2 for o in range(SIDE)]
    pz = [(d + o) & 3 for o in range(SIDE)]
    apart = sum(jnp.where(c == 2, 2, jnp.where(c == 0, 0, 1)) for c in (d >> 4, (d >> 2) & 3, d & 3))
    opens = jnp.where(apart <= NEAR, 3, jnp.where(apart >= FAR, 1, 2))

    barrier = pltpu.get_barrier_semaphore()
    for dy, dx in GROUPS:
        for dz in ALONG_Z:
            pl.semaphore_signal(barrier, inc=1, device_id=(1 - m, py[dy] + px[dx] + pz[dz]), device_id_type=MESH)
    deltas = sorted({s * k for s in (1, -1) for k in (1, rot, rot + 1, rot - 1) if k})
    for delta in deltas:
        pl.semaphore_signal(barrier, inc=1, device_id=(m, near(delta)), device_id_type=MESH)

    for copy in loads[:3]:
        copy.wait()
    turn = (slots - rot * CAP) % slots

    def turned(x):
        return jnp.where(m == 0, pltpu.roll(x, turn, axis=1), x)

    SB[...] = turned(SB[...])
    SC[0] = turned(SC[0])
    for i in range(3):
        SF[:, i * slots : (i + 1) * slots] = turned(SF[:, i * slots : (i + 1) * slots])

    def hat(count, at, frac):
        i = iota((count, GROUP), 0)
        return jnp.where(i == at, 1.0 - frac, jnp.where(i == at + 1, frac, 0.0))

    def weigh(g):
        cols = pl.ds(pl.multiple_of(g * GROUP, GROUP), GROUP)
        b = SB[:, cols]
        fz, fx, fy = (SF[:, pl.ds(pl.multiple_of(i * slots + g * GROUP, GROUP), GROUP)] for i in range(3))
        hx, hy = hat(CX, (b >> 5) & 7, fx), hat(CY, b & 31, fy)
        for i in range(CX):
            w = hx[i : i + 1] * hy
            hi = w.astype(BF)
            WH[i * CY : (i + 1) * CY, cols] = hi
            WL[i * CY : (i + 1) * CY, cols] = (w - hi.astype(F32)).astype(BF)
        WZ[:, cols] = hat(CZ, b >> 8, fz)

    def split(h, x):
        hi = x.astype(BF)
        A3[:, h * LANES : (h + 1) * LANES] = hi
        A3[:, PLANE + h * LANES : PLANE + (h + 1) * LANES] = (x - hi.astype(F32)).astype(BF)

    lane1 = iota((CZ, LANES), 1)
    y4 = lane1 & 31
    fringe = (y4 == 0) | (y4 == CY - 1)

    def pack(it, get):
        sl, sr = get(0, 0), pltpu.roll(get(1, 0), 32, axis=1)
        for f in range(1, 4):
            here = (lane1 >> 5) == f
            sl = jnp.where(here, pltpu.roll(get(0, f), 32 * f, axis=1), sl)
            sr = jnp.where(here, pltpu.roll(get(1, f), (32 * f + 32) % 128, axis=1), sr)
        sendH[it, 0] = sl
        sendH[it, 1] = sr

    def rows_of(h, f):
        return slice((h * 4 + f) * PITCH, (h * 4 + f) * PITCH + CZ)

    BLOCKS = [(h, f) for h in range(2) for f in range(4)]

    def new(h, f):
        return jnp.where(fringe, FR[rows_of(h, f)], V[rows_of(h, f)])

    def at(z):
        return pl.ds(z, 8, stride=PITCH)

    top, low = CZ // 2 - 1, CZ // 2

    def solve(V):
        def forward(i, carry):
            a, b = carry
            for u in range(8):
                z = i * 8 + u
                a = (R[at(z)] + a) * G[at(z)]
                b = (R[at(CZ - 1 - z)] + b) * G[at(CZ - 1 - z)]
                D[at(z)] = a
                D[at(CZ - 1 - z)] = b
            return a, b

        zero = jnp.zeros((8, LANES), F32)
        a, b = lax.fori_loop(0, CZ // 16, forward, (zero, zero))
        a = (a + G[at(top)] * b) * MID[...]
        b = b + G[at(low)] * a
        V[at(top)] = a
        V[at(low)] = b

        def backward(i, carry):
            a, b = carry
            for u in range(9):
                z = i * 9 + u + 1
                a = D[at(top - z)] + G[at(top - z)] * a
                b = D[at(low + z)] + G[at(low + z)] * b
                V[at(top - z)] = a
                V[at(low + z)] = b
            return a, b

        lax.fori_loop(0, 7, backward, (a, b))

    def from_within():
        NS[...] = jnp.dot(A3[...], NN[...], preferred_element_type=F32)
        for h, f in BLOCKS:
            x = NS[f * CZ : (f + 1) * CZ, h * LANES : (h + 1) * LANES]
            R[rows_of(h, f)] = IN[rows_of(h, f)] + CS[rows_of(h, f)] * x

    loads[3].wait()
    pack(0, lambda h, f: F0[f * CZ : (f + 1) * CZ, h * LANES : (h + 1) * LANES])
    for h in range(2):
        split(h, F0[:, h * LANES : (h + 1) * LANES])

    early = pltpu.make_async_remote_copy(
        src_ref=VE, dst_ref=GOT, send_sem=m_sem.at[0], recv_sem=m_sem.at[1],
        device_id=(m, near(rot)), device_id_type=MESH,
    )
    carried = [
        pltpu.make_async_remote_copy(
            src_ref=src, dst_ref=dst, send_sem=m_sem.at[2 + 2 * i], recv_sem=m_sem.at[3 + 2 * i],
            device_id=(m, near(rot)), device_id_type=MESH,
        )
        for i, (src, dst) in enumerate(((SC.at[0], SC.at[1]), *((CARRY.at[k], CARRY.at[3 + k]) for k in range(3))))
    ]

    def packing(h):
        c = lane1 & 63
        inner = (((c - 32) >> 1) + (1 - h)) * CY + jnp.where(c & 1 == 0, 1, CY - 2)
        return jnp.where(c < 32, c + 96 * h, inner & 127)

    def unpacking(h):
        x, y = lane1 >> 5, lane1 & 31
        outer = x == 3 * h
        place = jnp.where(outer, y, 32 + (x - (1 - h)) * 2 + (y >> 4)) + 64 * h
        return place & 127, outer | (y == 1) | (y == CY - 2)

    def gather(x, index):
        return jnp.take_along_axis(x, index, axis=1, mode="promise_in_bounds")

    planes = [(KV, 0, 1.0), (KV, CZ, 1.0), (SV, 0, 1000.0)]

    @pl.when(moved)
    def _():
        for copy in loads[4:]:
            copy.wait()
        for k, (ref, r, _) in enumerate(planes):
            a, b = (gather(ref[0, r : r + CZ, h * LANES : (h + 1) * LANES], packing(h)) for h in range(2))
            CARRY[k] = jnp.where(lane1 < 64, a, b)

    @pl.loop(0, ITERS)
    def _(it):
        ahead = (it > 0) & moved
        edge = [(sendH.at[it, e], recvH.at[it, e]) for e in range(2)]

        def halo(e, delta):
            return pltpu.make_async_remote_copy(
                src_ref=edge[e][0], dst_ref=edge[e][1],
                send_sem=hs_sem.at[it, e], recv_sem=hr_sem.at[it, e],
                device_id=(m, near(delta)), device_id_type=MESH,
            )

        def part(u):
            rows = pl.ds(u * PITCH, PITCH)
            return pltpu.make_async_remote_copy(
                src_ref=VE.at[rows], dst_ref=GOT.at[rows], send_sem=m_sem.at[0], recv_sem=m_sem.at[1],
                device_id=(m, near(rot)), device_id_type=MESH,
            )

        def chunk_at(t):
            return (CHUNKS >> (4 * t)) & 15

        lag = jnp.where((it > 0) & (m == 0), (rot + 1) // 4, 0)

        def group(k):
            dy, dx = (packed([g[0] for g in GROUPS]) >> (2 * k)) & 3, (packed([g[1] for g in GROUPS]) >> (2 * k)) & 3
            return ((((d >> 4) + dy) & 3) * 4 + (((d >> 2) + dx) & 3) - lag) & (n // SIDE - 1)

        per = TILE // GROUP
        shift = jnp.where((it > 0) & (m == 0), rot, 0)

        def send(t):
            for j in range(per):
                g = group(t * per + j)
                for dz in ALONG_Z:
                    pltpu.make_async_remote_copy(
                        src_ref=sendS.at[it, pz[dz] & 1, g * 2 + (pz[dz] >> 1)], dst_ref=recvS.at[it, d],
                        send_sem=s_sem.at[it], recv_sem=r_sem.at[it],
                        device_id=(1 - m, (g * SIDE + pz[dz] + shift) & (n - 1)), device_id_type=MESH,
                    ).start()

        @pl.loop(0, tiles)
        def _(t):
            @pl.when((it == 0) & (t == opens))
            def _():
                pl.semaphore_wait(barrier, n + len(deltas))

                @pl.loop(0, opens - 1)
                def _(u):
                    send(u)

            @pl.when((it == 0) & (t == opens))
            def _():
                halo(0, -1).start()
                halo(1, 1).start()

            @pl.when(((it > 0) & (t > 0)) | (t >= opens))
            def _():
                send(t - 1)

            @pl.when((it > 0) & (t == 0))
            def _():
                pack(it, new)

            @pl.when((it > 0) & (t == 0) & (m == 0))
            def _():
                halo(0, -1).start()
                halo(1, 1).start()

            @pl.when(ahead & (t == 0))
            def _():
                if rot == 1:
                    pltpu.make_async_copy(edge[0][0], edge[0][1], hr_sem.at[it, 0]).start()
                else:
                    halo(0, rot - 1).start()
                halo(1, rot + 1).start()
                from_within()
                for k in range(8):
                    VE[k * PITCH + CZ : (k + 1) * PITCH] = jnp.zeros((PITCH - CZ, LANES), F32)
                solve(VE)
                R[...] = jnp.zeros_like(R)

            @pl.when((it == 0) & (t == 3) & moved)
            def _():
                carried[0].start()
                carried[1].start()

            @pl.when(ahead)
            def _():
                @pl.loop(chunk_at(t), chunk_at(t + 1))
                def _(u):
                    part(u).start()

            @pl.when((it == 0) & (t == 0))
            def _():
                pl.loop(0, n // SIDE)(weigh)

            cols = [pl.ds(pl.multiple_of(group(t * per + j) * GROUP, GROUP), GROUP) for j in range(per)]

            def gathered(ref):
                return jnp.concatenate([ref[:, c] for c in cols], axis=1)

            wh = gathered(WH)
            a3 = jnp.concatenate([A3[...], A3[:, :PLANE]], axis=1)
            p = jnp.dot(a3, jnp.concatenate([wh, wh, gathered(WL)], axis=0), preferred_element_type=F32)
            s = jnp.sum(p.reshape(4, CZ, TILE) * gathered(WZ)[None], axis=1)
            first = iota((2, LANES), 1) < CAP
            for j in range(per):
                g = group(t * per + j)
                for i in range(2):
                    x = s[:, j * GROUP + i * LANES : j * GROUP + (i + 1) * LANES]
                    y = pltpu.roll(x, CAP, axis=1)
                    sendS[it, 0, g * 2 + i] = jnp.where(first, x[:2], y[2:])
                    sendS[it, 1, g * 2 + i] = jnp.where(first, y[:2], x[2:])

        send(tiles - 1)

        @pl.when(ahead)
        def _():
            @pl.loop(chunk_at(tiles), 8)
            def _(u):
                part(u).start()

        @pl.when((it == 0) & moved)
        def _():
            carried[2].start()
            carried[3].start()

        @pl.when((it == 0) & (m == 0))
        def _():
            for copy in loads[4:]:
                copy.wait()
            GOT[...] = jnp.zeros_like(GOT)

        @pl.when(it == 0)
        def _():
            src, dst = iota((512, 256), 0) & 255, iota((512, 256), 1)
            gap = jnp.abs(src - dst)
            sy, dy = src & 31, dst & 31
            rim = (sy == 0) | (sy == CY - 1) | (dy == 0) | (dy == CY - 1)
            NN[...] = jnp.where(((gap == 1) | (gap == CY)) & ~rim, 1.0, 0.0).astype(BF)

        @pl.when(ahead)
        def _():
            for copy in carried:
                copy.wait()
            for k, (ref, r, other) in enumerate(planes):
                for h in range(2):
                    index, used = unpacking(h)
                    ref[1, r : r + CZ, h * LANES : (h + 1) * LANES] = jnp.where(used, gather(CARRY[3 + k], index), other)

        @pl.when((it == 0) | moved)
        def _():
            @pl.loop(0, n // SIDE)
            def _(g):
                cols = pl.ds(pl.multiple_of(g * GROUP, GROUP), GROUP)
                c = SC[it, :, cols]
                ZO[:, cols] = jnp.where(iota((CZ, GROUP), 0) == (c >> 8), 1.0, 0.0).astype(BF)
                cq = ((c >> 5) & 7) * 2 + jnp.where((c & 31) == 0, 0, 1)
                QO[:, cols] = jnp.where(iota((16, GROUP), 0) == cq, 1.0, 0.0)

            for h in range(2):
                lanes = slice(h * LANES, (h + 1) * LANES)
                inv = 1.0 / SV[it, :, lanes]
                for f in range(4):
                    k = f // 3
                    c = KV[it, k * CZ : (k + 1) * CZ, lanes]
                    EP[rows_of(h, f)] = (1.0 + 4.0 * c) * inv
                    CS[rows_of(h, f)] = c * inv
                    IN[rows_of(h, f)] = F0[f * CZ : (f + 1) * CZ, lanes] * inv

            def factor(i, carry):
                ha, hb = carry
                for u in range(8):
                    z = i * 8 + u
                    ta, tb = EP[at(z)] + ha, EP[at(CZ - 1 - z)] + hb
                    ga, gb = 1.0 / (1.0 + ta), 1.0 / (1.0 + tb)
                    G[at(z)] = ga
                    G[at(CZ - 1 - z)] = gb
                    ha, hb = ta * ga, tb * gb
                return ha, hb

            one = jnp.ones((8, LANES), F32)
            ha, hb = lax.fori_loop(0, CZ // 16, factor, (one, one))
            MID[...] = 1.0 / (ha + hb - ha * hb)

        @pl.when(jnp.logical_not(ahead))
        def _():
            from_within()

        for e in range(2):
            halo(e, 1).wait_recv()
        halo(1, 1).wait_send()
        if rot == 1:

            @pl.when(jnp.logical_not(ahead))
            def _():
                halo(0, 1).wait_send()
        else:
            halo(0, 1).wait_send()
        hr, hl = recvH[it, 0], recvH[it, 1]
        for h, f in BLOCKS:
            if h == 0:
                x = jnp.where(lane1 < 32, pltpu.roll(hl, (128 - 32 * f) % 128, axis=1), 0.0)
            else:
                x = jnp.where(lane1 >= 96, pltpu.roll(hr, 96 - 32 * f, axis=1), 0.0)
            R[rows_of(h, f)] = R[rows_of(h, f)] + CS[rows_of(h, f)] * x

        pltpu.make_async_copy(recvS.at[it], recvS.at[it], r_sem.at[it]).wait()
        got = recvS[it].reshape(n // 4, 8, LANES)
        front = (iota(got.shape, 1) & 2) == 0
        turned = pltpu.roll(got, CAP, axis=2)
        turned = jnp.where(front, pltpu.roll(turned, 6, axis=1), pltpu.roll(turned, 2, axis=1))
        rest = jnp.where((iota(got.shape, 2) < CAP) == front, got, turned).reshape(2 * n, LANES)
        for piece in range(2):
            part = rest.astype(BF).astype(F32)
            rest = rest - part
            V2[piece] = part
        for i in range(n // 2):
            cols = slice(i * LANES, (i + 1) * LANES)
            for piece in range(2):
                for f in range(4):
                    r = piece * 64 + f * 16
                    QV[r : r + 16, cols] = (QO[:, cols] * V2[piece, i * 4 + f : i * 4 + f + 1]).astype(BF)
        dp = lax.dot_general(ZO[...], QV[...], (((1,), (1,)), ((), ())), preferred_element_type=F32)
        dp = dp + pltpu.roll(dp, CAP, axis=1)
        column = (lane1 >> 5) * 2 + (y4 >> 4)
        beside = (y4 == 1) | (y4 == CY - 2)
        for h, f in BLOCKS:
            x = gather(dp, column + (f * 16 + h * 8))
            FR[rows_of(h, f)] = x
            R[rows_of(h, f)] = R[rows_of(h, f)] + jnp.where(beside, CS[rows_of(h, f)] * x, 0.0)
        solve(V)

        pltpu.make_async_copy(recvS.at[it], recvS.at[it], s_sem.at[it]).wait()

        @pl.when(it < ITERS - 1)
        def _():
            for h in range(2):
                split(h, jnp.concatenate([new(h, f) for f in range(4)], axis=0))

    @pl.when(moved)
    def _():
        early.wait()

    for h, f in BLOCKS:
        out[f * CZ : (f + 1) * CZ, h * LANES : (h + 1) * LANES] = jnp.where(
            fringe, FR[rows_of(h, f)], V[rows_of(h, f)] + GOT[rows_of(h, f)]
        )


def step(rot, n, args):
    slots = n * CAP
    vm = pltpu.VMEM
    dma = pltpu.SemaphoreType.DMA
    tall = vm((8 * PITCH, LANES), F32)
    return pl.pallas_call(
        functools.partial(kernel, rot, n),
        out_shape=jax.ShapeDtypeStruct((4 * CZ, PLANE), F32),
        in_specs=[pl.BlockSpec(memory_space=pl.ANY)] * 6,
        out_specs=pl.BlockSpec(memory_space=pltpu.VMEM),
        scratch_shapes=[
            vm((512, 256), F32), vm((2, 256, 256), F32), vm((2, 128, 256), F32),
            vm((1, slots), jnp.int32), vm((1, 3 * slots), F32), vm((2, 1, slots), jnp.int32),
            vm((512, 512), BF), vm((256, slots), BF), vm((256, slots), BF), vm((CZ, slots), F32), vm((CZ, slots), BF),
            vm((16, slots), F32), vm((128, slots), BF), vm((512, 256), BF),
            vm((2, 2 * n, LANES), F32),
            tall, tall, tall, tall, tall, tall, tall, tall,
            vm((512, 256), F32), tall, tall, vm((8, LANES), F32), vm((6, CZ, LANES), F32),
            vm((ITERS, 2, n // 2, 2, LANES), F32), vm((ITERS, n, 2, LANES), F32),
            vm((ITERS, 2, CZ, LANES), F32), vm((ITERS, 2, CZ, LANES), F32),
            dma((6,)), dma((ITERS,)), dma((ITERS,)), dma((ITERS, 2)), dma((ITERS, 2)), dma((10,)),
        ],
        compiler_params=pltpu.CompilerParams(collective_id=rot, has_side_effects=True),
        name=f"rotor_step_{rot}",
    )(*args)


def solution(mesh):
    n = mesh.shape["blk"]

    def local(rotation_step, field_state, diffusivity, stretch, donor_base, donor_frac, fringe_cell):
        slots = n * CAP
        args = (
            field_state.reshape(4 * CZ, PLANE),
            diffusivity.reshape(2 * CZ, PLANE),
            stretch.reshape(CZ, PLANE),
            donor_base.reshape(1, slots),
            donor_frac.reshape(1, 3 * slots),
            fringe_cell.reshape(1, slots),
        )
        branches = [functools.partial(lambda rot, a: step(rot, n, a), rot) for rot in range(1, TURN_MOST + 1)]
        new = lax.switch(jnp.clip(rotation_step[0] - 1, 0, TURN_MOST - 1), branches, args)
        return new.reshape(1, 1, 4, CZ, PLANE)

    placed = (
        P(),
        P("mesh", "blk", None, None, None),
        P("mesh", "blk", None, None, None),
        P("mesh", "blk", None, None),
        P("mesh", "blk", None),
        P("mesh", "blk", None, None),
        P("mesh", "blk", None),
    )
    return jax.shard_map(
        local, mesh=mesh, in_specs=placed,
        out_specs=P("mesh", "blk", None, None, None), check_vma=False,
    )
```

```python
import functools

import jax
import jax.numpy as jnp
from jax import lax
from jax.experimental import pallas as pl
from jax.experimental.pallas import tpu as pltpu
from jax.sharding import PartitionSpec as P

CX, CY, CZ = 8, 32, 128
PLANE = CX * CY
ITERS = 2
TURN_MOST = 7
CAP = 64
TILE = 1024
SIDE = 4
GROUPS = sorted(
    ((dy, dx) for dy in range(SIDE) for dx in range(SIDE)),
    key=lambda o: -sum(min(a, SIDE - a) for a in o),
)
ALONG_Z = (2, 1, 3, 0)
NEAR, FAR = 2, 5
CHUNKS = 0x64210
GROUP = SIDE * CAP


def packed(values):
    word = sum(v << (2 * i) for i, v in enumerate(values))
    return word - (1 << 32) if word >= 1 << 31 else word

LANES = 128
PITCH = 132
MESH = pl.DeviceIdType.MESH
BF = jnp.bfloat16
F32 = jnp.float32


def iota(shape, dim):
    return lax.broadcasted_iota(jnp.int32, shape, dim)


def kernel(
    rot, n,
    fs, kap, st, db, df, fc, out,
    F0, KV, SV, SB, SF, SC, A3, WH, WL, WZ, ZO, QO, QV, NN, V2,
    EP, CS, IN, R, G, D, V, FR, NS, VE, GOT, MID, CARRY,
    sendS, recvS, sendH, recvH,
    in_sem, s_sem, r_sem, hs_sem, hr_sem, m_sem,
):
    m = lax.axis_index("mesh")
    d = lax.axis_index("blk")
    slots = n * CAP
    tiles = slots // TILE
    moved = m == 1

    def near(delta):
        return (d + delta) & (n - 1)

    loads = [
        pltpu.make_async_copy(src, dst, in_sem.at[i])
        for i, (src, dst) in enumerate(
            ((db, SB), (df, SF), (fc, SC.at[0]), (fs, F0), (kap, KV.at[0]), (st, SV.at[0]))
        )
    ]
    for copy in loads:
        copy.start()

    py = [(((d >> 4) + o) & 3) << 4 for o in range(SIDE)]
    px = [(((d >> 2) + o) & 3) << 2 for o in range(SIDE)]
    pz = [(d + o) & 3 for o in range(SIDE)]
    apart = sum(jnp.where(c == 2, 2, jnp.where(c == 0, 0, 1)) for c in (d >> 4, (d >> 2) & 3, d & 3))
    opens = jnp.where(apart <= NEAR, 3, jnp.where(apart >= FAR, 1, 2))

    barrier = pltpu.get_barrier_semaphore()
    for dy, dx in GROUPS:
        for dz in ALONG_Z:
            pl.semaphore_signal(barrier, inc=1, device_id=(1 - m, py[dy] + px[dx] + pz[dz]), device_id_type=MESH)
    deltas = sorted({s * k for s in (1, -1) for k in (1, rot, rot + 1, rot - 1) if k})
    for delta in deltas:
        pl.semaphore_signal(barrier, inc=1, device_id=(m, near(delta)), device_id_type=MESH)

    for copy in loads[:3]:
        copy.wait()
    turn = (slots - rot * CAP) % slots

    def turned(x):
        return jnp.where(m == 0, pltpu.roll(x, turn, axis=1), x)

    SB[...] = turned(SB[...])
    SC[0] = turned(SC[0])
    for i in range(3):
        SF[:, i * slots : (i + 1) * slots] = turned(SF[:, i * slots : (i + 1) * slots])

    def hat(count, at, frac):
        i = iota((count, GROUP), 0)
        return jnp.where(i == at, 1.0 - frac, jnp.where(i == at + 1, frac, 0.0))

    def weigh(g):
        cols = pl.ds(pl.multiple_of(g * GROUP, GROUP), GROUP)
        b = SB[:, cols]
        fz, fx, fy = (SF[:, pl.ds(pl.multiple_of(i * slots + g * GROUP, GROUP), GROUP)] for i in range(3))
        hx, hy = hat(CX, (b >> 5) & 7, fx), hat(CY, b & 31, fy)
        for i in range(CX):
            w = hx[i : i + 1] * hy
            hi = w.astype(BF)
            WH[i * CY : (i + 1) * CY, cols] = hi
            WL[i * CY : (i + 1) * CY, cols] = (w - hi.astype(F32)).astype(BF)
        WZ[:, cols] = hat(CZ, b >> 8, fz)

    def split(h, x):
        hi = x.astype(BF)
        A3[:, h * LANES : (h + 1) * LANES] = hi
        A3[:, PLANE + h * LANES : PLANE + (h + 1) * LANES] = (x - hi.astype(F32)).astype(BF)

    lane1 = iota((CZ, LANES), 1)
    y4 = lane1 & 31
    fringe = (y4 == 0) | (y4 == CY - 1)

    def pack(it, get):
        sl, sr = get(0, 0), pltpu.roll(get(1, 0), 32, axis=1)
        for f in range(1, 4):
            here = (lane1 >> 5) == f
            sl = jnp.where(here, pltpu.roll(get(0, f), 32 * f, axis=1), sl)
            sr = jnp.where(here, pltpu.roll(get(1, f), (32 * f + 32) % 128, axis=1), sr)
        sendH[it, 0] = sl
        sendH[it, 1] = sr

    def rows_of(h, f):
        return slice((h * 4 + f) * PITCH, (h * 4 + f) * PITCH + CZ)

    BLOCKS = [(h, f) for h in range(2) for f in range(4)]

    def new(h, f):
        return jnp.where(fringe, FR[rows_of(h, f)], V[rows_of(h, f)])

    def at(z):
        return pl.ds(z, 8, stride=PITCH)

    top, low = CZ // 2 - 1, CZ // 2

    def solve(V):
        def forward(i, carry):
            a, b = carry
            for u in range(8):
                z = i * 8 + u
                a = (R[at(z)] + a) * G[at(z)]
                b = (R[at(CZ - 1 - z)] + b) * G[at(CZ - 1 - z)]
                D[at(z)] = a
                D[at(CZ - 1 - z)] = b
            return a, b

        zero = jnp.zeros((8, LANES), F32)
        a, b = lax.fori_loop(0, CZ // 16, forward, (zero, zero))
        a = (a + G[at(top)] * b) * MID[...]
        b = b + G[at(low)] * a
        V[at(top)] = a
        V[at(low)] = b

        def backward(i, carry):
            a, b = carry
            for u in range(9):
                z = i * 9 + u + 1
                a = D[at(top - z)] + G[at(top - z)] * a
                b = D[at(low + z)] + G[at(low + z)] * b
                V[at(top - z)] = a
                V[at(low + z)] = b
            return a, b

        lax.fori_loop(0, 7, backward, (a, b))

    def from_within():
        NS[...] = jnp.dot(A3[...], NN[...], preferred_element_type=F32)
        for h, f in BLOCKS:
            x = NS[f * CZ : (f + 1) * CZ, h * LANES : (h + 1) * LANES]
            R[rows_of(h, f)] = IN[rows_of(h, f)] + CS[rows_of(h, f)] * x

    loads[3].wait()
    pack(0, lambda h, f: F0[f * CZ : (f + 1) * CZ, h * LANES : (h + 1) * LANES])
    for h in range(2):
        split(h, F0[:, h * LANES : (h + 1) * LANES])

    early = pltpu.make_async_remote_copy(
        src_ref=VE, dst_ref=GOT, send_sem=m_sem.at[0], recv_sem=m_sem.at[1],
        device_id=(m, near(rot)), device_id_type=MESH,
    )
    carried = [
        pltpu.make_async_remote_copy(
            src_ref=src, dst_ref=dst, send_sem=m_sem.at[2 + 2 * i], recv_sem=m_sem.at[3 + 2 * i],
            device_id=(m, near(rot)), device_id_type=MESH,
        )
        for i, (src, dst) in enumerate(((SC.at[0], SC.at[1]), *((CARRY.at[k], CARRY.at[3 + k]) for k in range(3))))
    ]

    def packing(h):
        c = lane1 & 63
        inner = (((c - 32) >> 1) + (1 - h)) * CY + jnp.where(c & 1 == 0, 1, CY - 2)
        return jnp.where(c < 32, c + 96 * h, inner & 127)

    def unpacking(h):
        x, y = lane1 >> 5, lane1 & 31
        outer = x == 3 * h
        place = jnp.where(outer, y, 32 + (x - (1 - h)) * 2 + (y >> 4)) + 64 * h
        return place & 127, outer | (y == 1) | (y == CY - 2)

    def gather(x, index):
        return jnp.take_along_axis(x, index, axis=1, mode="promise_in_bounds")

    planes = [(KV, 0, 1.0), (KV, CZ, 1.0), (SV, 0, 1000.0)]

    @pl.when(moved)
    def _():
        for copy in loads[4:]:
            copy.wait()
        for k, (ref, r, _) in enumerate(planes):
            a, b = (gather(ref[0, r : r + CZ, h * LANES : (h + 1) * LANES], packing(h)) for h in range(2))
            CARRY[k] = jnp.where(lane1 < 64, a, b)

    @pl.loop(0, ITERS)
    def _(it):
        ahead = (it > 0) & moved
        edge = [(sendH.at[it, e], recvH.at[it, e]) for e in range(2)]

        def halo(e, delta):
            return pltpu.make_async_remote_copy(
                src_ref=edge[e][0], dst_ref=edge[e][1],
                send_sem=hs_sem.at[it, e], recv_sem=hr_sem.at[it, e],
                device_id=(m, near(delta)), device_id_type=MESH,
            )

        def part(u):
            rows = pl.ds(u * PITCH, PITCH)
            return pltpu.make_async_remote_copy(
                src_ref=VE.at[rows], dst_ref=GOT.at[rows], send_sem=m_sem.at[0], recv_sem=m_sem.at[1],
                device_id=(m, near(rot)), device_id_type=MESH,
            )

        def chunk_at(t):
            return (CHUNKS >> (4 * t)) & 15

        lag = jnp.where((it > 0) & (m == 0), (rot + 1) // 4, 0)

        def group(k):
            dy, dx = (packed([g[0] for g in GROUPS]) >> (2 * k)) & 3, (packed([g[1] for g in GROUPS]) >> (2 * k)) & 3
            return ((((d >> 4) + dy) & 3) * 4 + (((d >> 2) + dx) & 3) - lag) & (n // SIDE - 1)

        per = TILE // GROUP
        shift = jnp.where((it > 0) & (m == 0), rot, 0)

        def send(t):
            for j in range(per):
                g = group(t * per + j)
                for dz in ALONG_Z:
                    pltpu.make_async_remote_copy(
                        src_ref=sendS.at[it, pz[dz] & 1, g * 2 + (pz[dz] >> 1)], dst_ref=recvS.at[it, d],
                        send_sem=s_sem.at[it], recv_sem=r_sem.at[it],
                        device_id=(1 - m, (g * SIDE + pz[dz] + shift) & (n - 1)), device_id_type=MESH,
                    ).start()

        @pl.loop(0, tiles)
        def _(t):
            @pl.when((it == 0) & (t == opens))
            def _():
                pl.semaphore_wait(barrier, n + len(deltas))

                @pl.loop(0, opens - 1)
                def _(u):
                    send(u)

            @pl.when((it == 0) & (t == opens))
            def _():
                halo(0, -1).start()
                halo(1, 1).start()

            @pl.when(((it > 0) & (t > 0)) | (t >= opens))
            def _():
                send(t - 1)

            @pl.when((it > 0) & (t == 0))
            def _():
                pack(it, new)

            @pl.when((it > 0) & (t == 0) & (m == 0))
            def _():
                halo(0, -1).start()
                halo(1, 1).start()

            @pl.when(ahead & (t == 0))
            def _():
                if rot == 1:
                    pltpu.make_async_copy(edge[0][0], edge[0][1], hr_sem.at[it, 0]).start()
                else:
                    halo(0, rot - 1).start()
                halo(1, rot + 1).start()
                from_within()
                for k in range(8):
                    VE[k * PITCH + CZ : (k + 1) * PITCH] = jnp.zeros((PITCH - CZ, LANES), F32)
                solve(VE)
                R[...] = jnp.zeros_like(R)

            @pl.when((it == 0) & (t == 3) & moved)
            def _():
                carried[0].start()
                carried[1].start()

            @pl.when(ahead)
            def _():
                @pl.loop(chunk_at(t), chunk_at(t + 1))
                def _(u):
                    part(u).start()

            @pl.when((it == 0) & (t == 0))
            def _():
                pl.loop(0, n // SIDE)(weigh)

            cols = [pl.ds(pl.multiple_of(group(t * per + j) * GROUP, GROUP), GROUP) for j in range(per)]

            def gathered(ref):
                return jnp.concatenate([ref[:, c] for c in cols], axis=1)

            wh = gathered(WH)
            a3 = jnp.concatenate([A3[...], A3[:, :PLANE]], axis=1)
            p = jnp.dot(a3, jnp.concatenate([wh, wh, gathered(WL)], axis=0), preferred_element_type=F32)
            s = jnp.sum(p.reshape(4, CZ, TILE) * gathered(WZ)[None], axis=1)
            first = iota((2, LANES), 1) < CAP
            for j in range(per):
                g = group(t * per + j)
                for i in range(2):
                    x = s[:, j * GROUP + i * LANES : j * GROUP + (i + 1) * LANES]
                    y = pltpu.roll(x, CAP, axis=1)
                    sendS[it, 0, g * 2 + i] = jnp.where(first, x[:2], y[2:])
                    sendS[it, 1, g * 2 + i] = jnp.where(first, y[:2], x[2:])

        send(tiles - 1)

        @pl.when(ahead)
        def _():
            @pl.loop(chunk_at(tiles), 8)
            def _(u):
                part(u).start()

        @pl.when((it == 0) & moved)
        def _():
            carried[2].start()
            carried[3].start()

        @pl.when((it == 0) & (m == 0))
        def _():
            for copy in loads[4:]:
                copy.wait()
            GOT[...] = jnp.zeros_like(GOT)

        @pl.when(it == 0)
        def _():
            src, dst = iota((512, 256), 0) & 255, iota((512, 256), 1)
            gap = jnp.abs(src - dst)
            sy, dy = src & 31, dst & 31
            rim = (sy == 0) | (sy == CY - 1) | (dy == 0) | (dy == CY - 1)
            NN[...] = jnp.where(((gap == 1) | (gap == CY)) & ~rim, 1.0, 0.0).astype(BF)

        @pl.when(ahead)
        def _():
            for copy in carried:
                copy.wait()
            for k, (ref, r, other) in enumerate(planes):
                for h in range(2):
                    index, used = unpacking(h)
                    ref[1, r : r + CZ, h * LANES : (h + 1) * LANES] = jnp.where(used, gather(CARRY[3 + k], index), other)

        @pl.when((it == 0) | moved)
        def _():
            @pl.loop(0, n // SIDE)
            def _(g):
                cols = pl.ds(pl.multiple_of(g * GROUP, GROUP), GROUP)
                c = SC[it, :, cols]
                ZO[:, cols] = jnp.where(iota((CZ, GROUP), 0) == (c >> 8), 1.0, 0.0).astype(BF)
                cq = ((c >> 5) & 7) * 2 + jnp.where((c & 31) == 0, 0, 1)
                QO[:, cols] = jnp.where(iota((16, GROUP), 0) == cq, 1.0, 0.0)

            for h in range(2):
                lanes = slice(h * LANES, (h + 1) * LANES)
                inv = 1.0 / SV[it, :, lanes]
                for f in range(4):
                    k = f // 3
                    c = KV[it, k * CZ : (k + 1) * CZ, lanes]
                    EP[rows_of(h, f)] = (1.0 + 4.0 * c) * inv
                    CS[rows_of(h, f)] = c * inv
                    IN[rows_of(h, f)] = F0[f * CZ : (f + 1) * CZ, lanes] * inv

            def factor(i, carry):
                ha, hb = carry
                for u in range(8):
                    z = i * 8 + u
                    ta, tb = EP[at(z)] + ha, EP[at(CZ - 1 - z)] + hb
                    ga, gb = 1.0 / (1.0 + ta), 1.0 / (1.0 + tb)
                    G[at(z)] = ga
                    G[at(CZ - 1 - z)] = gb
                    ha, hb = ta * ga, tb * gb
                return ha, hb

            one = jnp.ones((8, LANES), F32)
            ha, hb = lax.fori_loop(0, CZ // 16, factor, (one, one))
            MID[...] = 1.0 / (ha + hb - ha * hb)

        @pl.when(jnp.logical_not(ahead))
        def _():
            from_within()

        for e in range(2):
            halo(e, 1).wait_recv()
        halo(1, 1).wait_send()
        if rot == 1:

            @pl.when(jnp.logical_not(ahead))
            def _():
                halo(0, 1).wait_send()
        else:
            halo(0, 1).wait_send()
        hr, hl = recvH[it, 0], recvH[it, 1]
        for h, f in BLOCKS:
            if h == 0:
                x = jnp.where(lane1 < 32, pltpu.roll(hl, (128 - 32 * f) % 128, axis=1), 0.0)
            else:
                x = jnp.where(lane1 >= 96, pltpu.roll(hr, 96 - 32 * f, axis=1), 0.0)
            R[rows_of(h, f)] = R[rows_of(h, f)] + CS[rows_of(h, f)] * x

        pltpu.make_async_copy(recvS.at[it], recvS.at[it], r_sem.at[it]).wait()
        got = recvS[it].reshape(n // 4, 8, LANES)
        front = (iota(got.shape, 1) & 2) == 0
        turned = pltpu.roll(got, CAP, axis=2)
        turned = jnp.where(front, pltpu.roll(turned, 6, axis=1), pltpu.roll(turned, 2, axis=1))
        rest = jnp.where((iota(got.shape, 2) < CAP) == front, got, turned).reshape(2 * n, LANES)
        for piece in range(2):
            part = rest.astype(BF).astype(F32)
            rest = rest - part
            V2[piece] = part
        for i in range(n // 2):
            cols = slice(i * LANES, (i + 1) * LANES)
            for piece in range(2):
                for f in range(4):
                    r = piece * 64 + f * 16
                    QV[r : r + 16, cols] = jnp.where(QO[:, cols] > 0.5, V2[piece, i * 4 + f : i * 4 + f + 1], 0.0).astype(BF)
        dp = lax.dot_general(ZO[...], QV[...], (((1,), (1,)), ((), ())), preferred_element_type=F32)
        dp = dp + pltpu.roll(dp, CAP, axis=1)
        column = (lane1 >> 5) * 2 + (y4 >> 4)
        beside = (y4 == 1) | (y4 == CY - 2)
        for h, f in BLOCKS:
            x = gather(dp, column + (f * 16 + h * 8))
            FR[rows_of(h, f)] = x
            R[rows_of(h, f)] = R[rows_of(h, f)] + jnp.where(beside, CS[rows_of(h, f)] * x, 0.0)
        solve(V)

        pltpu.make_async_copy(recvS.at[it], recvS.at[it], s_sem.at[it]).wait()

        @pl.when(it < ITERS - 1)
        def _():
            for h in range(2):
                split(h, jnp.concatenate([new(h, f) for f in range(4)], axis=0))

    @pl.when(moved)
    def _():
        early.wait()

    for h, f in BLOCKS:
        out[f * CZ : (f + 1) * CZ, h * LANES : (h + 1) * LANES] = jnp.where(
            fringe, FR[rows_of(h, f)], V[rows_of(h, f)] + GOT[rows_of(h, f)]
        )


def step(rot, n, args):
    slots = n * CAP
    vm = pltpu.VMEM
    dma = pltpu.SemaphoreType.DMA
    tall = vm((8 * PITCH, LANES), F32)
    return pl.pallas_call(
        functools.partial(kernel, rot, n),
        out_shape=jax.ShapeDtypeStruct((4 * CZ, PLANE), F32),
        in_specs=[pl.BlockSpec(memory_space=pl.ANY)] * 6,
        out_specs=pl.BlockSpec(memory_space=pltpu.VMEM),
        scratch_shapes=[
            vm((512, 256), F32), vm((2, 256, 256), F32), vm((2, 128, 256), F32),
            vm((1, slots), jnp.int32), vm((1, 3 * slots), F32), vm((2, 1, slots), jnp.int32),
            vm((512, 512), BF), vm((256, slots), BF), vm((256, slots), BF), vm((CZ, slots), F32), vm((CZ, slots), BF),
            vm((16, slots), F32), vm((128, slots), BF), vm((512, 256), BF),
            vm((2, 2 * n, LANES), F32),
            tall, tall, tall, tall, tall, tall, tall, tall,
            vm((512, 256), F32), tall, tall, vm((8, LANES), F32), vm((6, CZ, LANES), F32),
            vm((ITERS, 2, n // 2, 2, LANES), F32), vm((ITERS, n, 2, LANES), F32),
            vm((ITERS, 2, CZ, LANES), F32), vm((ITERS, 2, CZ, LANES), F32),
            dma((6,)), dma((ITERS,)), dma((ITERS,)), dma((ITERS, 2)), dma((ITERS, 2)), dma((10,)),
        ],
        compiler_params=pltpu.CompilerParams(collective_id=rot, has_side_effects=True),
        name=f"rotor_step_{rot}",
    )(*args)


def solution(mesh):
    n = mesh.shape["blk"]

    def local(rotation_step, field_state, diffusivity, stretch, donor_base, donor_frac, fringe_cell):
        slots = n * CAP
        args = (
            field_state.reshape(4 * CZ, PLANE),
            diffusivity.reshape(2 * CZ, PLANE),
            stretch.reshape(CZ, PLANE),
            donor_base.reshape(1, slots),
            donor_frac.reshape(1, 3 * slots),
            fringe_cell.reshape(1, slots),
        )
        branches = [functools.partial(lambda rot, a: step(rot, n, a), rot) for rot in range(1, TURN_MOST + 1)]
        new = lax.switch(jnp.clip(rotation_step[0] - 1, 0, TURN_MOST - 1), branches, args)
        return new.reshape(1, 1, 4, CZ, PLANE)

    placed = (
        P(),
        P("mesh", "blk", None, None, None),
        P("mesh", "blk", None, None, None),
        P("mesh", "blk", None, None),
        P("mesh", "blk", None),
        P("mesh", "blk", None, None),
        P("mesh", "blk", None),
    )
    return jax.shard_map(
        local, mesh=mesh, in_specs=placed,
        out_specs=P("mesh", "blk", None, None, None), check_vma=False,
    )
```
